256 devices in a mesh: seqa: 16 (over x_lo, y, core), seqb: 16 (over x_hi, z).
Axes of the slice: x: 4 (x_hi: 2, x_lo: 2; x = x_hi * 2 + x_lo), y: 4, z: 8, core: 2. Of those that a mesh axis runs over, the one named last changes fastest.
Arguments:
- hidden_in: bfloat16 [32768, 2880], P(('seqa', 'seqb')), may hold values from -6 to 6
- queries: bfloat16 [32768, 4096], P(('seqa', 'seqb')), may hold values from -200 to 200
- grad_out: bfloat16 [32768, 4096], P(('seqa', 'seqb')), may hold values from -5 to 5
- key_weight: bfloat16 [2880, 512], P(None, ('seqa', 'seqb')), may hold values from -0.109375 to 0.109375
- value_weight: bfloat16 [2880, 512], P(None, ('seqa', 'seqb')), may hold values from -0.109375 to 0.109375
Outputs:
- grad_queries: bfloat16 [32768, 4096], P(('seqa', 'seqb'))
- grad_keys: bfloat16 [32768, 512], P(('seqa', 'seqb'))
- grad_values: bfloat16 [32768, 512], P(('seqa', 'seqb'))
- grad_inputs: bfloat16 [32768, 2880], P(('seqa', 'seqb'))
- grad_key_weight: float32 [2880, 512], P(None, ('seqa', 'seqb'))
- grad_value_weight: float32 [2880, 512], P(None, ('seqa', 'seqb'))
The draws below stay inside these ranges and needn't reach their ends.
All inputs are finite; a program needn't handle non-finite values.
Results may differ from the reference program's by a relative error of at most 0.011.
Values may be sent and summed in bfloat16 or wider, within the bound.
A program may use at most 128 MiB of HBM per device.

```python
import jax
import jax.numpy as jnp
from jax import lax

D = 2880
KV_HEADS = 8
HEAD = 64
WIN = 128
TOK_DEV = 128
TOKENS = 32768
QW = 4096
KVW = 512


def draw_queries(key, part):
    base = jnp.clip(jax.random.normal(key, (TOKENS, QW), jnp.float32), -5.0, 5.0)
    return base.astype(jnp.bfloat16)


def draw_grad_out(key, part):
    base = jnp.clip(jax.random.normal(jax.random.fold_in(key, 7), (TOKENS, QW), jnp.float32), -5.0, 5.0)
    return base.astype(jnp.bfloat16)


def steps_of(rng, dims, shards, smallest, high):
    gain = 1.0
    for position, parts in shards:
        steps = jax.random.uniform(jax.random.fold_in(jax.random.fold_in(rng, 6), position), (parts,), jnp.float32, smallest / len(shards), high / len(shards))
        gain = gain * jnp.repeat(jnp.exp(steps), dims[position] // parts).reshape((-1,) + (1,) * (len(dims) - 1 - position))
    return gain


def centred(stream_key, shape, scale, bound, shards=(), held_as=jnp.bfloat16):
    loudness = steps_of(stream_key, shape, shards, -0.22, 0.18) if shards else 1.0
    entries = jax.random.normal(stream_key, shape, jnp.float32) * scale * loudness
    return jnp.minimum(jnp.maximum(entries, -bound), bound).astype(held_as)


def setup_inputs(seed: int = 0) -> dict:
    streams_of = jax.random.split(jax.random.key(seed), 6)
    hidden_in = centred(streams_of[0], (TOKENS, D), 1.0, 6.0, ((0, 256),))
    queries = draw_queries(jax.random.fold_in(streams_of[5], 71), 0)
    grad_out = draw_grad_out(jax.random.fold_in(streams_of[5], 71), 0)
    key_weight = centred(streams_of[3], (D, KVW), D ** -0.5, 0.109375, ((1, 256),))
    value_weight = centred(streams_of[4], (D, KVW), D ** -0.5, 0.109375, ((1, 256),))
    return dict(hidden_in=hidden_in, queries=queries, grad_out=grad_out, key_weight=key_weight, value_weight=value_weight)


def lowered(value):
    return lax.optimization_barrier(value.astype(jnp.bfloat16))


def head_group(query_rows, grad_rows, key_rows, value_rows, allowed):
    count = query_rows.shape[0]
    width = key_rows.shape[1]
    group = query_rows.shape[1] // width
    factor = width ** -0.5
    query_heads = query_rows.reshape(count, group, width).astype(jnp.float32)
    grad_heads = grad_rows.reshape(count, group, width).astype(jnp.float32)
    key_wide = key_rows.astype(jnp.float32)
    value_wide = value_rows.astype(jnp.float32)
    scores = jnp.einsum("tgh,lh->gtl", query_heads, key_wide) * factor
    masked = jnp.where(allowed[None], scores, -1e30)
    peak = jnp.max(masked, axis=2, keepdims=True)
    weights = jnp.where(allowed[None], jnp.exp(masked - peak), 0.0)
    weights = weights / jnp.sum(weights, axis=2, keepdims=True)
    weights_low = lowered(weights).astype(jnp.float32)
    attended = lowered(jnp.einsum("gtl,lh->tgh", weights_low, value_wide)).astype(jnp.float32)
    delta = jnp.sum(grad_heads * attended, axis=2)
    grad_weights = jnp.einsum("tgh,lh->gtl", grad_heads, value_wide)
    grad_scores = lowered(weights * (grad_weights - jnp.transpose(delta)[:, :, None])).astype(jnp.float32)
    grad_query = jnp.einsum("gtl,lh->tgh", grad_scores, key_wide) * factor
    grad_key = jnp.einsum("gtl,tgh->lh", grad_scores, query_heads) * factor
    grad_value = jnp.einsum("gtl,tgh->lh", weights_low, grad_heads)
    return grad_query.reshape(count, group * width).astype(jnp.bfloat16), grad_key, grad_value


def reference(hidden_in, queries, grad_out, key_weight, value_weight):
    keys_all = jnp.dot(hidden_in, key_weight, preferred_element_type=jnp.float32).astype(jnp.bfloat16)
    values_all = jnp.dot(hidden_in, value_weight, preferred_element_type=jnp.float32).astype(jnp.bfloat16)
    front = jnp.zeros((WIN, KVW), keys_all.dtype)
    padded_keys = jnp.concatenate([front, keys_all], axis=0)
    padded_values = jnp.concatenate([front, values_all], axis=0)
    span = TOK_DEV + WIN

    def one_block(index):
        start = (index * TOK_DEV).astype(jnp.int32)
        query_rows = lax.dynamic_slice_in_dim(queries, start, TOK_DEV, 0)
        grad_rows = lax.dynamic_slice_in_dim(grad_out, start, TOK_DEV, 0)
        key_rows = lax.dynamic_slice_in_dim(padded_keys, start, span, 0)
        value_rows = lax.dynamic_slice_in_dim(padded_values, start, span, 0)
        query_pos = start + jnp.arange(TOK_DEV, dtype=jnp.int32)
        key_pos = start - WIN + jnp.arange(span, dtype=jnp.int32)
        gap = query_pos[:, None] - key_pos[None, :]
        allowed = (gap >= 0) & (gap <= WIN) & (key_pos[None, :] >= 0)
        query_groups = jnp.moveaxis(query_rows.reshape(TOK_DEV, KV_HEADS, -1), 1, 0)
        grad_groups = jnp.moveaxis(grad_rows.reshape(TOK_DEV, KV_HEADS, -1), 1, 0)
        key_groups = jnp.moveaxis(key_rows.reshape(span, KV_HEADS, HEAD), 1, 0)
        value_groups = jnp.moveaxis(value_rows.reshape(span, KV_HEADS, HEAD), 1, 0)
        grad_query, grad_key, grad_value = lax.map(
            lambda items: head_group(items[0], items[1], items[2], items[3], allowed),
            (query_groups, grad_groups, key_groups, value_groups))
        return (jnp.moveaxis(grad_query, 0, 1).reshape(TOK_DEV, QW),
                jnp.moveaxis(grad_key, 0, 1).reshape(span, KVW),
                jnp.moveaxis(grad_value, 0, 1).reshape(span, KVW))

    block_count = TOKENS // TOK_DEV
    grad_query, grad_key, grad_value = lax.map(one_block, jnp.arange(block_count, dtype=jnp.int32))

    def combine(blocks):
        own_part = blocks[:, WIN:]
        later = jnp.concatenate([blocks[1:, :WIN], jnp.zeros_like(blocks[:1, :WIN])], axis=0)
        merged = jnp.concatenate([own_part[:, :TOK_DEV - WIN], own_part[:, TOK_DEV - WIN:] + later], axis=1)
        return merged.reshape(TOKENS, KVW).astype(jnp.bfloat16)

    grad_queries = grad_query.reshape(TOKENS, QW)
    grad_keys = combine(grad_key)
    grad_values = combine(grad_value)
    contract_cols = (((1,), (1,)), ((), ()))
    grad_inputs = (lax.dot_general(grad_keys, key_weight, contract_cols, preferred_element_type=jnp.float32)
                   + lax.dot_general(grad_values, value_weight, contract_cols, preferred_element_type=jnp.float32)).astype(jnp.bfloat16)
    contract_rows = (((0,), (0,)), ((), ()))
    grad_scale = TOKENS ** -0.5
    grad_key_weight = lax.dot_general(hidden_in, grad_keys, contract_rows, preferred_element_type=jnp.float32) * grad_scale
    grad_value_weight = lax.dot_general(hidden_in, grad_values, contract_rows, preferred_element_type=jnp.float32) * grad_scale
    return grad_queries, grad_keys, grad_values, grad_inputs, grad_key_weight, grad_value_weight
```

```python
import functools

import jax
import jax.numpy as jnp
from jax import lax
from jax.experimental import pallas as pl
from jax.experimental.pallas import tpu as pltpu
from jax.sharding import PartitionSpec as P

KV_HEADS = 8
HEAD = 64
WIN = 128
D = 2880
LANE_CUT = 1408
NT = (((1,), (1,)), ((), ()))
NN = (((1,), (0,)), ((), ()))
MESH = pl.DeviceIdType.MESH
BF16 = jnp.bfloat16
F32 = jnp.float32


def coords():
    a = lax.axis_index("seqa")
    b = lax.axis_index("seqb")
    x_lo = a // 8
    y = lax.rem(a // 2, 4)
    core = lax.rem(a, 2)
    x_hi = b // 8
    z = lax.rem(b, 8)
    return x_hi * 2 + x_lo, y, z, core


def at(x, y, z, core):
    return (lax.rem(x, 2) * 8 + y * 2 + core, (x // 2) * 8 + z)


def along(step):
    a = lax.axis_index("seqa")
    b = lax.axis_index("seqb")
    index = lax.rem(a * 16 + b + step + 256, 256)
    return (index // 16, lax.rem(index, 16))


def partners():
    x, y, z, core = coords()
    found = [at(x, y, lax.rem(z + k, 8), core) for k in range(1, 8)]
    found += [at(lax.rem(x + k, 4), y, z, core) for k in (1, 3)]
    found += [at(x, lax.rem(y + k, 4), z, core) for k in (1, 3)]
    found += [at(x, y, z, 1 - core), along(1), along(-1)]
    return found


def meet():
    barrier = pltpu.get_barrier_semaphore()
    found = partners()
    for device in found:
        pl.semaphore_signal(barrier, inc=1, device_id=device, device_id_type=MESH)
    pl.semaphore_wait(barrier, len(found))


def send(src, dst, send_sem, recv_sem, device):
    copy = pltpu.make_async_remote_copy(
        src_ref=src, dst_ref=dst, send_sem=send_sem, recv_sem=recv_sem, device_id=device, device_id_type=MESH
    )
    copy.start()
    return copy


def gather_kernel(
    ws, ht, wk, wv, kk, vv, pair, zg, tk, tv, zsem, zrem, ks, kr, vs, vr, cs, cr, hs, hr, ms, mr, own_sem
):
    x, y, z, core = coords()
    x_lo, x_hi = lax.rem(x, 2), x // 2
    meet()
    zc = []
    for k in range(1, 8):
        zc.append(send(ws, zg.at[z], zsem.at[k], zrem.at[k], at(x, y, lax.rem(z + k, 8), core)))
    other = at(x, y, z, 1 - core)
    hc = send(ht, pair.at[core], hs, hr, other)
    mine = pltpu.make_async_copy(ht, pair.at[core], own_sem)
    mine.start()
    zg[z] = ws[...]
    for c in zc:
        c.wait()
    for i in range(8):
        rows = zg[i].astype(F32)
        tk[2 * i : 2 * i + 2] = rows[0:2]
        tv[2 * i : 2 * i + 2] = rows[2:4]
    wk[x_lo, y, core, x_hi] = tk[...].astype(BF16)
    wv[x_lo, y, core, x_hi] = tv[...].astype(BF16)

    xp, xm = lax.rem(x + 1, 4), lax.rem(x + 3, 4)
    yp, ym = lax.rem(y + 1, 4), lax.rem(y + 3, 4)
    xo, yo = lax.rem(x + 2, 4), lax.rem(y + 2, 4)
    dxp, dxm = at(xp, y, z, core), at(xm, y, z, core)
    dyp, dym = at(x, yp, z, core), at(x, ym, z, core)

    def k1(q):
        return wk.at[lax.rem(q, 2), y, core, q // 2]

    def v1(q):
        return wv.at[x_lo, q, core, x_hi]

    def cut(view, half):
        return view.at[:, :LANE_CUT] if half == 0 else view.at[:, LANE_CUT:]

    ka = send(k1(x), k1(x), ks.at[0], kr.at[0], dxp)
    kb = send(k1(x), k1(x), ks.at[1], kr.at[1], dxm)
    va = send(v1(y), v1(y), vs.at[0], vr.at[0], dyp)
    vb = send(v1(y), v1(y), vs.at[1], vr.at[1], dym)
    ka.wait_recv()
    kc = send(cut(k1(xm), 0), cut(k1(xm), 0), ks.at[2], kr.at[2], dxp)
    va.wait_recv()
    vc = send(cut(v1(ym), 0), cut(v1(ym), 0), vs.at[2], vr.at[2], dyp)
    kb.wait_recv()
    kd = send(cut(k1(xp), 1), cut(k1(xp), 1), ks.at[3], kr.at[3], dxm)
    vb.wait_recv()
    vd = send(cut(v1(yp), 1), cut(v1(yp), 1), vs.at[3], vr.at[3], dym)
    sent = [ka, kb, kc, kd, va, vb, vc, vd]
    kc.wait_recv()
    kd.wait_recv()

    def k2(q):
        return wk.at[:, q, core]

    def k2h(q, half):
        return wk.at[half, q, core]

    def v2(q):
        return wv.at[lax.rem(q, 2), :, core, q // 2]

    def v2h(q, half):
        return wv.at[lax.rem(q, 2), 2 * half : 2 * half + 2, core, q // 2]

    ke = send(k2(y), k2(y), ks.at[4], kr.at[4], dyp)
    kf = send(k2(y), k2(y), ks.at[5], kr.at[5], dym)
    vc.wait_recv()
    vd.wait_recv()
    ve = send(v2(x), v2(x), vs.at[4], vr.at[4], dxp)
    vf = send(v2(x), v2(x), vs.at[5], vr.at[5], dxm)
    across = [send(k2(y), k2(y), cs.at[0], cr.at[0], other), send(v2(x), v2(x), cs.at[1], cr.at[1], other)]
    ke.wait_recv()
    kg = send(k2h(ym, 0), k2h(ym, 0), ks.at[6], kr.at[6], dyp)
    across.append(send(k2(ym), k2(ym), cs.at[2], cr.at[2], other))
    kf.wait_recv()
    kh = send(k2h(yp, 1), k2h(yp, 1), ks.at[7], kr.at[7], dym)
    across.append(send(k2(yp), k2(yp), cs.at[3], cr.at[3], other))
    ve.wait_recv()
    vg = send(v2h(xm, 0), v2h(xm, 0), vs.at[6], vr.at[6], dxp)
    across.append(send(v2(xm), v2(xm), cs.at[4], cr.at[4], other))
    vf.wait_recv()
    vh = send(v2h(xp, 1), v2h(xp, 1), vs.at[7], vr.at[7], dxm)
    across.append(send(v2(xp), v2(xp), cs.at[5], cr.at[5], other))
    kg.wait_recv()
    kh.wait_recv()
    across.append(send(k2(yo), k2(yo), cs.at[6], cr.at[6], other))
    vg.wait_recv()
    vh.wait_recv()
    across.append(send(v2(xo), v2(xo), cs.at[7], cr.at[7], other))
    for c in across:
        c.wait_recv()
    nxt = along(1)
    halos = []
    for i, (w, out) in enumerate(((wk, kk), (wv, vv))):
        flat = w[...].reshape(512, D)
        proj = lax.dot_general(flat, ht[...], NN, preferred_element_type=F32)
        out[128:256] = jnp.transpose(proj).astype(BF16)
        halos.append(send(out.at[128:256], out.at[0:128], ms.at[i], mr.at[i], nxt))
    for c in halos:
        c.wait()
    hc.wait()
    mine.wait()
    for c in sent + [ke, kf, kg, kh, ve, vf, vg, vh] + across:
        c.wait_send()


def gather(ws, ht):
    full = jax.ShapeDtypeStruct((2, 4, 2, 2, 16, D), BF16)
    rows = jax.ShapeDtypeStruct((256, 512), BF16)
    dma = pltpu.SemaphoreType.DMA
    vm = pl.BlockSpec(memory_space=pltpu.VMEM)
    return pl.pallas_call(
        gather_kernel,
        out_shape=(full, full, rows, rows, jax.ShapeDtypeStruct((2, D, 128), BF16)),
        in_specs=[vm] * 2,
        out_specs=(vm,) * 5,
        scratch_shapes=[
            pltpu.VMEM((8, 4, D), BF16),
            pltpu.VMEM((16, D), F32),
            pltpu.VMEM((16, D), F32),
            dma((8,)),
            dma((8,)),
            dma((8,)),
            dma((8,)),
            dma((8,)),
            dma((8,)),
            dma((8,)),
            dma((8,)),
            dma(()),
            dma(()),
            dma((2,)),
            dma((2,)),
            dma(()),
        ],
        compiler_params=pltpu.CompilerParams(collective_id=0, has_side_effects=True, vmem_limit_bytes=56 * 2**20),
        name="gather",
    )(ws, ht)


def attention_kernel(kb, vb, qb, gb, dq, own, prior, bias, ds_s, pl_s, q_s, g_s):
    factor = HEAD ** (-0.5)
    log2e = 1.4426950408889634
    first = (lax.axis_index("seqa") + lax.axis_index("seqb")) == 0
    s_pos = lax.broadcasted_iota(jnp.int32, (256, 128), 0)
    t_pos = lax.broadcasted_iota(jnp.int32, (256, 128), 1)
    gap = t_pos + 128 - s_pos
    start = jnp.where(first, 128, 0)
    bias[...] = jnp.where((gap >= 0) & (gap <= WIN) & (s_pos >= start), 0.0, -1e30).astype(F32)
    dks, dvs = [], []
    for jj in range(2):
        kj = kb[:, 64 * jj : 64 * jj + 64]
        vj = vb[:, 64 * jj : 64 * jj + 64]
        kt = jnp.transpose(kj)
        outs = []
        for h in range(8):
            col = (jj * 8 + h) * 64
            q = qb[:, col : col + 64]
            g = gb[:, col : col + 64]
            q_s[128 * h : 128 * h + 128] = q
            g_s[128 * h : 128 * h + 128] = g
            s = lax.dot_general(kj, q, NT, preferred_element_type=F32) + bias[...]
            gp = lax.dot_general(vj, g, NT, preferred_element_type=F32)
            peak = jnp.max(s, axis=0, keepdims=True)
            e = jnp.exp2((s - peak) * (factor * log2e))
            total = jnp.sum(e, axis=0, keepdims=True)
            p = e * (1.0 / total)
            low = p.astype(BF16)
            delta = jnp.sum(low.astype(F32) * gp, axis=0, keepdims=True)
            ds = (p * (gp - delta)).astype(BF16)
            ds_s[:, 128 * h : 128 * h + 128] = ds
            pl_s[:, 128 * h : 128 * h + 128] = low
            outs.append(lax.dot_general(kt, ds, NN, preferred_element_type=F32) * factor)
            if h % 2 == 1:
                two = jnp.concatenate(outs[-2:], axis=0)
                dq[:, col - 64 : col + 64] = jnp.transpose(two).astype(BF16)
        dks.append(lax.dot_general(ds_s[...], q_s[...], NN, preferred_element_type=F32) * factor)
        dvs.append(lax.dot_general(pl_s[...], g_s[...], NN, preferred_element_type=F32))
    for i, parts in enumerate((dks, dvs)):
        both = jnp.concatenate(parts, axis=1)
        prior[i] = both[0:128].astype(BF16)
        own[i] = both[128:256]


def attention(keys, values, queries, grad_out):
    kv = pl.BlockSpec((256, 128), lambda j: (0, j))
    qg = pl.BlockSpec((128, 1024), lambda j: (0, j))
    part = pl.BlockSpec((2, 128, 128), lambda j: (0, 0, j))
    return pl.pallas_call(
        attention_kernel,
        grid=(4,),
        out_shape=(
            jax.ShapeDtypeStruct((128, 4096), BF16),
            jax.ShapeDtypeStruct((2, 128, 512), F32),
            jax.ShapeDtypeStruct((2, 128, 512), BF16),
        ),
        in_specs=[kv, kv, qg, qg],
        out_specs=(qg, part, part),
        scratch_shapes=[
            pltpu.VMEM((256, 128), F32),
            pltpu.VMEM((256, 1024), BF16),
            pltpu.VMEM((256, 1024), BF16),
            pltpu.VMEM((1024, 64), BF16),
            pltpu.VMEM((1024, 64), BF16),
        ],
        compiler_params=pltpu.CompilerParams(vmem_limit_bytes=40 * 2**20),
        name="attention",
    )(keys, values, queries, grad_out)


def scatter_kernel(
    own, prior, pair, wk_in, wv_in, gk, gv, git, dw,
    wk, wv, later, gboth, gsel, dk, dv,
    k1s, k1r, k2s, k2r, k3s, k3r, k4s, k4r, v1s, v1r, v2s, v2r, v3s, v3r, v4s, v4r,
    zs, zf, zr, wsem, psem, prem, csem, crem, ks, kr, vs, vr, zsem, zrem,
):
    x, y, z, core = coords()
    meet()
    pc = send(prior, later, psem, prem, along(-1))
    wc = [pltpu.make_async_copy(wk_in, wk, wsem.at[0]), pltpu.make_async_copy(wv_in, wv, wsem.at[1])]
    for c in wc:
        c.start()
    pc.wait()
    total_k = (own[0] + later[0].astype(F32)).astype(BF16)
    total_v = (own[1] + later[1].astype(F32)).astype(BF16)
    gk[...] = total_k
    gv[...] = total_v
    gboth[core, :, 0:512] = total_k
    gboth[core, :, 512:1024] = total_v
    cc = send(gboth.at[core], gboth.at[core], csem, crem, at(x, y, z, 1 - core))
    cc.wait()
    for c in range(2):
        turned = jnp.transpose(gboth[c].astype(F32)).astype(BF16)
        gsel[:, :, :, 128 * c : 128 * c + 128] = turned.reshape(16, 2, 32, 128)
    left = gsel[:, core].reshape(512, 256)
    right = jnp.concatenate([pair[0], pair[1]], axis=1)
    grads = lax.dot_general(left, right, NT, preferred_element_type=F32)
    dk[...] = grads[0:256].reshape(2, 4, 2, 16, D)
    dv[...] = grads[256:512].reshape(2, 4, 2, 16, D)

    xp, xm = lax.rem(x + 1, 4), lax.rem(x + 3, 4)
    yp, ym = lax.rem(y + 1, 4), lax.rem(y + 3, 4)
    xo, yo = lax.rem(x + 2, 4), lax.rem(y + 2, 4)
    dxp, dxm = at(xp, y, z, core), at(xm, y, z, core)
    dyp, dym = at(x, yp, z, core), at(x, ym, z, core)

    k1s[0] = dk[0, yo].astype(BF16)
    k1s[1] = dk[1, yo].astype(BF16)
    ka = send(k1s.at[0], k1r.at[0], ks.at[0], kr.at[0], dyp)
    kb = send(k1s.at[1], k1r.at[1], ks.at[1], kr.at[1], dym)
    xol, xoh = lax.rem(xo, 2), xo // 2
    v1s[0] = dv[xol, 0:2, xoh].astype(BF16)
    v1s[1] = dv[xol, 2:4, xoh].astype(BF16)
    va = send(v1s.at[0], v1r.at[0], vs.at[0], vr.at[0], dxp)
    vb = send(v1s.at[1], v1r.at[1], vs.at[1], vr.at[1], dxm)

    k2s[0, 1] = dk[1, yp].astype(BF16)
    k2s[1, 0] = dk[0, ym].astype(BF16)
    ka.wait_recv()
    k2s[0, 0] = (dk[0, yp] + k1r[0].astype(F32)).astype(BF16)
    kc = send(k2s.at[0], k2r.at[0], ks.at[2], kr.at[2], dyp)
    kb.wait_recv()
    k2s[1, 1] = (dk[1, ym] + k1r[1].astype(F32)).astype(BF16)
    kd = send(k2s.at[1], k2r.at[1], ks.at[3], kr.at[3], dym)

    xpl, xph, xml, xmh = lax.rem(xp, 2), xp // 2, lax.rem(xm, 2), xm // 2
    v2s[0, 2:4] = dv[xpl, 2:4, xph].astype(BF16)
    v2s[1, 0:2] = dv[xml, 0:2, xmh].astype(BF16)
    va.wait_recv()
    v2s[0, 0:2] = (dv[xpl, 0:2, xph] + v1r[0].astype(F32)).astype(BF16)
    vc = send(v2s.at[0], v2r.at[0], vs.at[2], vr.at[2], dxp)
    vb.wait_recv()
    v2s[1, 2:4] = (dv[xml, 2:4, xmh] + v1r[1].astype(F32)).astype(BF16)
    vd = send(v2s.at[1], v2r.at[1], vs.at[3], vr.at[3], dxm)

    for c in wc:
        c.wait()
    cols = lax.dot_general(gk[...], wk[...].reshape(512, D), NN, preferred_element_type=F32)
    cols += lax.dot_general(gv[...], wv[...].reshape(512, D), NN, preferred_element_type=F32)
    git[...] = jnp.transpose(cols).astype(BF16)

    kc.wait_recv()
    kd.wait_recv()
    dk[:, y] = dk[:, y] + k2r[0].astype(F32) + k2r[1].astype(F32)
    k3s[0] = dk[xol, y, xoh, :, :LANE_CUT].astype(BF16)
    k4s[2] = dk[xol, y, xoh].astype(BF16)
    ke = send(k3s.at[0], k3r.at[0], ks.at[4], kr.at[4], dxp)
    kf = send(k4s.at[2, :, LANE_CUT:], k4r.at[2, :, LANE_CUT:], ks.at[5], kr.at[5], dxm)
    x_lo, x_hi = lax.rem(x, 2), x // 2
    vc.wait_recv()
    vd.wait_recv()
    dv[x_lo, :, x_hi] = dv[x_lo, :, x_hi] + v2r[0].astype(F32) + v2r[1].astype(F32)
    v3s[0] = dv[x_lo, yo, x_hi, :, :LANE_CUT].astype(BF16)
    v4s[2] = dv[x_lo, yo, x_hi].astype(BF16)
    ve = send(v3s.at[0], v3r.at[0], vs.at[4], vr.at[4], dyp)
    vf = send(v4s.at[2, :, LANE_CUT:], v4r.at[2, :, LANE_CUT:], vs.at[5], vr.at[5], dym)

    k4s[0, :, LANE_CUT:] = dk[xpl, y, xph, :, LANE_CUT:].astype(BF16)
    k4s[1, :, :LANE_CUT] = dk[xml, y, xmh, :, :LANE_CUT].astype(BF16)
    v4s[0, :, LANE_CUT:] = dv[x_lo, yp, x_hi, :, LANE_CUT:].astype(BF16)
    v4s[1, :, :LANE_CUT] = dv[x_lo, ym, x_hi, :, :LANE_CUT].astype(BF16)
    ke.wait_recv()
    k4s[0, :, :LANE_CUT] = (dk[xpl, y, xph, :, :LANE_CUT] + k3r[0].astype(F32)).astype(BF16)
    kg = send(k4s.at[0], k4r.at[0], ks.at[6], kr.at[6], dxp)
    kf.wait_recv()
    k4s[1, :, LANE_CUT:] = (dk[xml, y, xmh, :, LANE_CUT:] + k4r[2, :, LANE_CUT:].astype(F32)).astype(BF16)
    kh = send(k4s.at[1], k4r.at[1], ks.at[7], kr.at[7], dxm)
    ve.wait_recv()
    v4s[0, :, :LANE_CUT] = (dv[x_lo, yp, x_hi, :, :LANE_CUT] + v3r[0].astype(F32)).astype(BF16)
    vg = send(v4s.at[0], v4r.at[0], vs.at[6], vr.at[6], dyp)
    vf.wait_recv()
    v4s[1, :, LANE_CUT:] = (dv[x_lo, ym, x_hi, :, LANE_CUT:] + v4r[2, :, LANE_CUT:].astype(F32)).astype(BF16)
    vh = send(v4s.at[1], v4r.at[1], vs.at[7], vr.at[7], dym)
    kg.wait_recv()
    kh.wait_recv()
    fk = dk[x_lo, y, x_hi] + k4r[0].astype(F32) + k4r[1].astype(F32)
    vg.wait_recv()
    vh.wait_recv()
    fv = dv[x_lo, y, x_hi] + v4r[0].astype(F32) + v4r[1].astype(F32)
    for i in range(8):
        zf[i, 0:2] = fk[2 * i : 2 * i + 2]
        zf[i, 2:4] = fv[2 * i : 2 * i + 2]
    zs[...] = zf[...].astype(BF16)
    zc = []
    for k in range(1, 8):
        to = lax.rem(z + k, 8)
        zc.append(send(zs.at[to], zr.at[k - 1], zsem.at[k], zrem.at[k], at(x, y, to, core)))
    total = zf[z]
    for k in range(7):
        zc[k].wait_recv()
        total = total + zr[k].astype(F32)
    dw[...] = total * (32768.0 ** (-0.5))
    for c in zc + [ka, kb, kc, kd, ke, kf, kg, kh, va, vb, vc, vd, ve, vf, vg, vh]:
        c.wait_send()


def scatter(own, prior, pair, wk, wv):
    dma = pltpu.SemaphoreType.DMA
    vm = pl.BlockSpec(memory_space=pltpu.VMEM)
    anyw = pl.BlockSpec(memory_space=pl.ANY)
    v = pltpu.VMEM
    ring_k = [v((2, 2, 16, D), BF16)] * 2 + [v((2, 2, 2, 16, D), BF16)] * 2
    ring_v = [v((2, 2, 16, D), BF16)] * 2 + [v((2, 4, 16, D), BF16)] * 2
    ring_end = [v((1, 16, LANE_CUT), BF16)] * 2 + [v((3, 16, D), BF16)] * 2
    return pl.pallas_call(
        scatter_kernel,
        out_shape=(
            jax.ShapeDtypeStruct((128, 512), BF16),
            jax.ShapeDtypeStruct((128, 512), BF16),
            jax.ShapeDtypeStruct((D, 128), BF16),
            jax.ShapeDtypeStruct((4, D), F32),
        ),
        in_specs=[vm, vm, vm, anyw, anyw],
        out_specs=(vm,) * 4,
        scratch_shapes=[
            v((2, 4, 2, 2, 16, D), BF16),
            v((2, 4, 2, 2, 16, D), BF16),
            v((2, 128, 512), BF16),
            v((2, 128, 1024), BF16),
            v((16, 2, 32, 256), BF16),
            v((2, 4, 2, 16, D), F32),
            v((2, 4, 2, 16, D), F32),
            *ring_k,
            *ring_end,
            *ring_v,
            *ring_end,
            v((8, 4, D), BF16),
            v((8, 4, D), F32),
            v((7, 4, D), BF16),
            dma((2,)),
            dma(()),
            dma(()),
            dma(()),
            dma(()),
            dma((8,)),
            dma((8,)),
            dma((8,)),
            dma((8,)),
            dma((8,)),
            dma((8,)),
        ],
        compiler_params=pltpu.CompilerParams(collective_id=1, has_side_effects=True, vmem_limit_bytes=60 * 2**20),
        name="scatter",
    )(own, prior, pair, wk, wv)


def shards(hidden_in, queries, grad_out, key_weight, value_weight):
    ws = jnp.concatenate([key_weight.T, value_weight.T], axis=0)
    wk, wv, keys, values, pair = gather(ws, hidden_in.T)
    grad_queries, own, prior = attention(keys, values, queries, grad_out)
    gk, gv, git, dw = scatter(own, prior, pair, wk, wv)
    return grad_queries, gk, gv, git.T, dw[0:2].T, dw[2:4].T


def solution(mesh):
    rows = P(("seqa", "seqb"), None)
    columns = P(None, ("seqa", "seqb"))
    return jax.shard_map(
        shards,
        mesh=mesh,
        in_specs=(rows, rows, rows, columns, columns),
        out_specs=(rows, rows, rows, rows, columns, columns),
        check_vma=False,
    )
```

```python
import jax
import jax.numpy as jnp
from jax import lax
from jax.experimental import pallas as pl
from jax.experimental.pallas import tpu as pltpu
from jax.sharding import PartitionSpec as P

KV_HEADS = 8
HEAD = 64
WIN = 128
D = 2880
LOW = (0, 640, 1408)
HIGH = (1408, 2176, 2880)
NT = (((1,), (1,)), ((), ()))
NN = (((1,), (0,)), ((), ()))
MESH = pl.DeviceIdType.MESH
BF16 = jnp.bfloat16
F32 = jnp.float32
FACTOR = HEAD ** (-0.5)
LOG2E = 1.4426950408889634


def coords():
    a = lax.axis_index("seqa")
    b = lax.axis_index("seqb")
    x_lo = a // 8
    y = lax.rem(a // 2, 4)
    core = lax.rem(a, 2)
    x_hi = b // 8
    z = lax.rem(b, 8)
    return x_hi * 2 + x_lo, y, z, core


def at(x, y, z, core):
    return (lax.rem(x, 2) * 8 + y * 2 + core, (x // 2) * 8 + z)


def along(step):
    a = lax.axis_index("seqa")
    b = lax.axis_index("seqb")
    index = lax.rem(a * 16 + b + step + 256, 256)
    return (index // 16, lax.rem(index, 16))


def meet():
    x, y, z, core = coords()
    found = [at(x, y, lax.rem(z + k, 8), core) for k in range(1, 8)]
    found += [at(lax.rem(x + k, 4), y, z, core) for k in (1, 3)]
    found += [at(x, lax.rem(y + k, 4), z, core) for k in (1, 3)]
    found += [at(x, y, z, 1 - core), along(1), along(-1)]
    barrier = pltpu.get_barrier_semaphore()
    for device in found:
        pl.semaphore_signal(barrier, inc=1, device_id=device, device_id_type=MESH)
    pl.semaphore_wait(barrier, len(found))


class Wire:
    def __init__(self, sems):
        self.sems, self.used, self.open = sems, 0, []

    def send(self, src, dst, device):
        copy = pltpu.make_async_remote_copy(
            src_ref=src,
            dst_ref=dst,
            send_sem=self.sems.at[self.used],
            recv_sem=self.sems.at[self.used + 1],
            device_id=device,
            device_id_type=MESH,
        )
        self.used += 2
        copy.start()
        self.open.append(copy)
        return copy

    def finish(self):
        for copy in self.open:
            copy.wait_send()


def gather_flow(wire, w, lanes, first):
    x, y, z, core = coords()
    x_lo, x_hi = lax.rem(x, 2), x // 2
    lo, mid, hi = lanes

    def block(axis, q, l0, l1):
        if axis == "x":
            return w.at[lax.rem(q, 2), y, core, q // 2, :, l0:l1]
        return w.at[x_lo, q, core, x_hi, :, l0:l1]

    def line(axis, q):
        if axis == "y":
            return w.at[:, q, core, :, :, lo:hi]
        return w.at[lax.rem(q, 2), :, core, q // 2, :, lo:hi]

    def half(axis, q, h):
        if axis == "y":
            return w.at[h, q, core, :, :, lo:hi]
        return w.at[lax.rem(q, 2), 2 * h : 2 * h + 2, core, q // 2, :, lo:hi]

    def ends(axis):
        p = x if axis == "x" else y
        plus, minus = lax.rem(p + 1, 4), lax.rem(p + 3, 4)
        if axis == "x":
            return p, plus, minus, at(plus, y, z, core), at(minus, y, z, core)
        return p, plus, minus, at(x, plus, z, core), at(x, minus, z, core)

    p, plus, minus, to_plus, to_minus = ends(first)
    own = block(first, p, lo, hi)
    a = wire.send(own, own, to_plus)
    b = wire.send(own, own, to_minus)
    yield
    a.wait_recv()
    c = wire.send(block(first, minus, lo, mid), block(first, minus, lo, mid), to_plus)
    b.wait_recv()
    d = wire.send(block(first, plus, mid, hi), block(first, plus, mid, hi), to_minus)
    yield
    c.wait_recv()
    d.wait_recv()
    second = "y" if first == "x" else "x"
    p, plus, minus, to_plus, to_minus = ends(second)
    opposite = lax.rem(p + 2, 4)
    other = at(x, y, z, 1 - core)
    a = wire.send(line(second, p), line(second, p), to_plus)
    b = wire.send(line(second, p), line(second, p), to_minus)
    across = [wire.send(line(second, p), line(second, p), other)]
    yield
    a.wait_recv()
    c = wire.send(half(second, minus, 0), half(second, minus, 0), to_plus)
    across.append(wire.send(line(second, minus), line(second, minus), other))
    b.wait_recv()
    d = wire.send(half(second, plus, 1), half(second, plus, 1), to_minus)
    across.append(wire.send(line(second, plus), line(second, plus), other))
    yield
    c.wait_recv()
    d.wait_recv()
    across.append(wire.send(line(second, opposite), line(second, opposite), other))
    yield
    for copy in across:
        copy.wait_recv()
    yield


def reduce_flow(wire, acc, fin, lanes, first, bufs):
    s1, r1, s2, r2, s3a, r3a, s3b, r3b, s4, r4 = bufs
    x, y, z, core = coords()
    x_lo, x_hi = lax.rem(x, 2), x // 2
    lo, mid, hi = lanes
    cut = mid - lo

    def half(q, h):
        if first == "y":
            return (h, q, slice(None), slice(None), slice(lo, hi))
        return (lax.rem(q, 2), slice(2 * h, 2 * h + 2), q // 2, slice(None), slice(lo, hi))

    def block(axis, q, l0, l1):
        if axis == "x":
            return (lax.rem(q, 2), y, q // 2, slice(None), slice(l0, l1))
        return (x_lo, q, x_hi, slice(None), slice(l0, l1))

    def ends(axis):
        p = x if axis == "x" else y
        plus, minus = lax.rem(p + 1, 4), lax.rem(p + 3, 4)
        if axis == "x":
            return p, plus, minus, at(plus, y, z, core), at(minus, y, z, core)
        return p, plus, minus, at(x, plus, z, core), at(x, minus, z, core)

    p, plus, minus, to_plus, to_minus = ends(first)
    opposite = lax.rem(p + 2, 4)
    s1[0] = acc[half(opposite, 0)].astype(BF16)
    s1[1] = acc[half(opposite, 1)].astype(BF16)
    a = wire.send(s1.at[0], r1.at[0], to_plus)
    b = wire.send(s1.at[1], r1.at[1], to_minus)
    s2[0, 1] = acc[half(plus, 1)].astype(BF16)
    s2[1, 0] = acc[half(minus, 0)].astype(BF16)
    yield
    a.wait_recv()
    s2[0, 0] = (acc[half(plus, 0)] + r1[0].astype(F32)).astype(BF16)
    c = wire.send(s2.at[0], r2.at[0], to_plus)
    b.wait_recv()
    s2[1, 1] = (acc[half(minus, 1)] + r1[1].astype(F32)).astype(BF16)
    d = wire.send(s2.at[1], r2.at[1], to_minus)
    yield
    c.wait_recv()
    d.wait_recv()
    for h in range(2):
        acc[half(p, h)] = acc[half(p, h)] + r2[0, h].astype(F32) + r2[1, h].astype(F32)
    second = "y" if first == "x" else "x"
    p, plus, minus, to_plus, to_minus = ends(second)
    opposite = lax.rem(p + 2, 4)
    s3a[...] = acc[block(second, opposite, lo, mid)].astype(BF16)
    s3b[...] = acc[block(second, opposite, mid, hi)].astype(BF16)
    a = wire.send(s3a, r3a, to_plus)
    b = wire.send(s3b, r3b, to_minus)
    s4[0, :, cut:] = acc[block(second, plus, mid, hi)].astype(BF16)
    s4[1, :, :cut] = acc[block(second, minus, lo, mid)].astype(BF16)
    yield
    a.wait_recv()
    s4[0, :, :cut] = (acc[block(second, plus, lo, mid)] + r3a[...].astype(F32)).astype(BF16)
    c = wire.send(s4.at[0], r4.at[0], to_plus)
    b.wait_recv()
    s4[1, :, cut:] = (acc[block(second, minus, mid, hi)] + r3b[...].astype(F32)).astype(BF16)
    d = wire.send(s4.at[1], r4.at[1], to_minus)
    yield
    c.wait_recv()
    d.wait_recv()
    fin[:, lo:hi] = acc[block(second, p, lo, hi)] + r4[0].astype(F32) + r4[1].astype(F32)
    yield


def flow_buffers(lanes):
    lo, mid, hi = lanes
    shapes = [(2, 2, 16, hi - lo)] * 2 + [(2, 2, 2, 16, hi - lo)] * 2
    shapes += [(16, mid - lo)] * 2 + [(16, hi - mid)] * 2 + [(2, 16, hi - lo)] * 2
    return [pltpu.VMEM(shape, BF16) for shape in shapes]


def step(*flows):
    for flow in flows:
        next(flow)


def kernel(ws_k, ws_v, ht, q_in, g_in, dq, gk, gv, git, dwk, dwv, *scratch):
    (
        zgk, zgv, tk, tv, wk, wv, hto, kt, vt, qv, gvm, qa, ga, pall, ds_s, bias, dqo,
        dko, dvo, dkp, dvp, dkl, dvl, gkt, gvt, gko, gvo, acc_k, acc_v, fin_k, fin_v,
        zsk, zsv, zrk, zrv, zfk, zfv,
    ) = scratch[:37]
    bufs = [scratch[37 + 10 * i : 47 + 10 * i] for i in range(4)]
    sems, local_sems = scratch[77:]
    x, y, z, core = coords()
    x_lo, x_hi = lax.rem(x, 2), x // 2
    other = at(x, y, z, 1 - core)
    before, after = along(-1), along(1)
    loads = [
        pltpu.make_async_copy(q_in, qv, local_sems.at[0]),
        pltpu.make_async_copy(g_in, gvm, local_sems.at[1]),
    ]
    for copy in loads:
        copy.start()
    meet()
    wire = Wire(sems)

    def spread(src, dst):
        return [wire.send(src, dst.at[z], at(x, y, lax.rem(z + k, 8), core)) for k in range(1, 8)]

    zk = spread(ws_k, zgk)
    zv = spread(ws_v, zgv)
    hc = wire.send(ht, hto, other)
    zgk[z] = ws_k[...]
    zgv[z] = ws_v[...]

    def assemble(copies, zg, rows, w):
        for copy in copies:
            copy.wait_recv()
        for i in range(8):
            rows[2 * i : 2 * i + 2] = zg[i].astype(F32)
        w[x_lo, y, core, x_hi] = rows[...].astype(BF16)

    assemble(zk, zgk, tk, wk)
    kl, kh = gather_flow(wire, wk, LOW, "x"), gather_flow(wire, wk, HIGH, "y")
    step(kl, kh)
    assemble(zv, zgv, tv, wv)
    vl, vh = gather_flow(wire, wv, LOW, "x"), gather_flow(wire, wv, HIGH, "y")
    step(kl, kh)

    first_device = (lax.axis_index("seqa") + lax.axis_index("seqb")) == 0
    s_pos = lax.broadcasted_iota(jnp.int32, (256, 128), 0)
    t_pos = lax.broadcasted_iota(jnp.int32, (256, 128), 1)
    gap = t_pos + 128 - s_pos
    allowed = (gap >= 0) & (gap <= WIN) & (s_pos >= jnp.where(first_device, 128, 0))
    bias[...] = jnp.where(allowed, 0.0, -1e30).astype(F32)
    step(kl, kh)
    step(vl, vh)
    for copy in loads:
        copy.wait()

    def stage(j, carry):
        for src, dst in ((qv, qa), (gvm, ga)):
            rows = src[:, pl.ds(pl.multiple_of(512 * j, 512), 512)]
            for h in range(8):
                dst[j, 128 * h : 128 * h + 128] = rows[:, 64 * h : 64 * h + 64]
        return carry

    lax.fori_loop(0, 8, stage, 0)
    step(kl, kh)
    step(vl, vh)
    step(kl, kh)
    step(vl, vh)

    def project(w, out, which):
        flat = w[:, :, which].reshape(256, D)
        rows = lax.dot_general(flat, ht[...], NN, preferred_element_type=F32)
        out[:, which, :, 128:256] = rows.astype(BF16).reshape(8, 32, 128)

    def pass_on(arr, c):
        return wire.send(arr.at[4 * c : 4 * c + 4, :, :, 128:256], arr.at[4 * c : 4 * c + 4, :, :, 0:128], after)

    def pass_back(arr, dst, c):
        return wire.send(arr.at[4 * c : 4 * c + 4], dst.at[4 * c : 4 * c + 4], before)

    project(wk, kt, core)
    step(kl, kh)
    project(wk, kt, 1 - core)
    k_halo = [pass_on(kt, 0), pass_on(kt, 1)]

    def forward(j, carry):
        kj = jnp.transpose(kt[j].reshape(64, 256))
        for pair in range(4):
            both = lax.dot_general(kj, qa[j, 256 * pair : 256 * pair + 256], NT, preferred_element_type=F32)
            for h in range(2):
                s = both[:, 128 * h : 128 * h + 128] + bias[...]
                peak = jnp.max(s, axis=0, keepdims=True)
                e = jnp.exp2((s - peak) * (FACTOR * LOG2E))
                p = e * (1.0 / jnp.sum(e, axis=0, keepdims=True))
                col = 256 * pair + 128 * h
                pall[j, :, col : col + 128] = p.astype(BF16)
        grad = jnp.transpose(lax.dot_general(pall[j], ga[j], NN, preferred_element_type=F32))
        dvp[j] = grad[:, 0:128].astype(BF16)
        dvo[j] = grad[:, 128:256]
        return carry

    def backward(j, carry):
        k_t = kt[j].reshape(64, 256)
        vj = jnp.transpose(vt[j].reshape(64, 256))
        for pair in range(4):
            both = lax.dot_general(vj, ga[j, 256 * pair : 256 * pair + 256], NT, preferred_element_type=F32)
            for h in range(2):
                col = 256 * pair + 128 * h
                gp = both[:, 128 * h : 128 * h + 128]
                p = pall[j, :, col : col + 128].astype(F32)
                delta = jnp.sum(p * gp, axis=0, keepdims=True)
                ds_s[:, col : col + 128] = (p * (gp - delta)).astype(BF16)
            turned = lax.dot_general(
                k_t, ds_s[:, 256 * pair : 256 * pair + 256], NN, preferred_element_type=F32
            )
            two = jnp.concatenate([turned[:, 0:128], turned[:, 128:256]], axis=0) * FACTOR
            at_col = pl.multiple_of(512 * j + 128 * pair, 128)
            dqo[:, pl.ds(at_col, 128)] = jnp.transpose(two).astype(BF16)
        grad = jnp.transpose(lax.dot_general(ds_s[...], qa[j], NN, preferred_element_type=F32)) * FACTOR
        dkp[j] = grad[:, 0:128].astype(BF16)
        dko[j] = grad[:, 128:256]
        return carry

    k_halo[0].wait_recv()
    lax.fori_loop(0, 4, forward, 0)
    dv_halo = [pass_back(dvp, dvl, 0)]
    step(vl, vh)
    k_halo[1].wait_recv()
    lax.fori_loop(4, 8, forward, 0)
    dv_halo.append(pass_back(dvp, dvl, 1))
    step(vl, vh)
    project(wv, vt, core)
    step(vl, vh)
    project(wv, vt, 1 - core)
    v_halo = [pass_on(vt, 0), pass_on(vt, 1)]

    def settle(halo, own, later, total, theirs):
        for copy in halo:
            copy.wait_recv()
        total[...] = (own[...] + later[...].astype(F32)).astype(BF16).reshape(8, 2, 32, 128)
        return wire.send(total.at[:, 1 - core], theirs, other)

    def weight_grad(total, theirs, acc):
        left = jnp.concatenate([total[:, core].reshape(256, 128), theirs[...].reshape(256, 128)], axis=1)
        right = jnp.concatenate([ht[...], hto[...]], axis=1)
        acc[...] = lax.dot_general(left, right, NT, preferred_element_type=F32).reshape(2, 4, 2, 16, D)

    swap_v = settle(dv_halo, dvo, dvl, gvt, gvo)
    v_halo[0].wait_recv()
    lax.fori_loop(0, 1, backward, 0)
    hc.wait_recv()
    swap_v.wait_recv()
    weight_grad(gvt, gvo, acc_v)
    rvl = reduce_flow(wire, acc_v, fin_v, LOW, "y", bufs[0])
    rvh = reduce_flow(wire, acc_v, fin_v, HIGH, "x", bufs[1])
    step(rvl, rvh)
    lax.fori_loop(1, 3, backward, 0)
    step(rvl, rvh)
    lax.fori_loop(3, 4, backward, 0)
    dk_halo = [pass_back(dkp, dkl, 0)]
    v_halo[1].wait_recv()
    lax.fori_loop(4, 6, backward, 0)
    step(rvl, rvh)
    lax.fori_loop(6, 7, backward, 0)
    step(rvl, rvh)
    lax.fori_loop(7, 8, backward, 0)
    dk_halo.append(pass_back(dkp, dkl, 1))
    stores = [pltpu.make_async_copy(dqo, dq, local_sems.at[2])]
    stores[0].start()
    step(rvl, rvh)

    def deal(fin, zf, zs, zr):
        for i in range(8):
            zf[i] = fin[2 * i : 2 * i + 2]
        zs[...] = zf[...].astype(BF16)
        copies = []
        for k in range(1, 8):
            to = lax.rem(z + k, 8)
            copies.append(wire.send(zs.at[to], zr.at[k - 1], at(x, y, to, core)))
        return copies

    def collect(copies, zf, zr, out):
        total = zf[z]
        for k in range(7):
            copies[k].wait_recv()
            total = total + zr[k].astype(F32)
        out[...] = total * (32768.0 ** (-0.5))

    deal_v = deal(fin_v, zfv, zsv, zrv)
    gv_rows = jnp.transpose(gvt[...].reshape(512, 128).astype(F32)).astype(BF16)
    gv[...] = gv_rows
    swap_k = settle(dk_halo, dko, dkl, gkt, gko)
    gk_rows = jnp.transpose(gkt[...].reshape(512, 128).astype(F32)).astype(BF16)
    gk[...] = gk_rows
    swap_k.wait_recv()
    weight_grad(gkt, gko, acc_k)
    rkl = reduce_flow(wire, acc_k, fin_k, LOW, "y", bufs[2])
    rkh = reduce_flow(wire, acc_k, fin_k, HIGH, "x", bufs[3])
    step(rkl, rkh)
    step(rkl, rkh)
    cols = lax.dot_general(gv[...], wv[...].reshape(512, D), NN, preferred_element_type=F32)
    cols += lax.dot_general(gk[...], wk[...].reshape(512, D), NN, preferred_element_type=F32)
    git[...] = jnp.transpose(cols).astype(BF16)
    collect(deal_v, zfv, zrv, dwv)
    step(rkl, rkh)
    step(rkl, rkh)
    step(rkl, rkh)
    deal_k = deal(fin_k, zfk, zsk, zrk)
    collect(deal_k, zfk, zrk, dwk)
    for copy in stores:
        copy.wait()
    wire.finish()


SEMS = 2 * (14 + 1 + 4 * 12 + 8 + 2 + 4 * 8 + 14)


def fused(ws_k, ws_v, ht, queries, grad_out):
    dma = pltpu.SemaphoreType.DMA
    vm = pl.BlockSpec(memory_space=pltpu.VMEM)
    hbm = pl.BlockSpec(memory_space=pl.ANY)
    v = pltpu.VMEM
    scratch = [
        v((8, 2, D), BF16), v((8, 2, D), BF16), v((16, D), F32), v((16, D), F32),
        v((2, 4, 2, 2, 16, D), BF16), v((2, 4, 2, 2, 16, D), BF16), v((D, 128), BF16),
        v((8, 2, 32, 256), BF16), v((8, 2, 32, 256), BF16), v((128, 4096), BF16), v((128, 4096), BF16),
        v((8, 1024, 64), BF16), v((8, 1024, 64), BF16), v((8, 256, 1024), BF16), v((256, 1024), BF16),
        v((256, 128), F32), v((128, 4096), BF16),
        v((8, 64, 128), F32), v((8, 64, 128), F32), v((8, 64, 128), BF16), v((8, 64, 128), BF16),
        v((8, 64, 128), BF16), v((8, 64, 128), BF16), v((8, 2, 32, 128), BF16), v((8, 2, 32, 128), BF16),
        v((8, 32, 128), BF16), v((8, 32, 128), BF16), v((2, 4, 2, 16, D), F32), v((2, 4, 2, 16, D), F32),
        v((16, D), F32), v((16, D), F32),
        v((8, 2, D), BF16), v((8, 2, D), BF16), v((7, 2, D), BF16), v((7, 2, D), BF16),
        v((8, 2, D), F32), v((8, 2, D), F32),
        *flow_buffers(LOW), *flow_buffers(HIGH), *flow_buffers(LOW), *flow_buffers(HIGH),
        dma((SEMS,)), dma((3,)),
    ]
    return pl.pallas_call(
        kernel,
        out_shape=(
            jax.ShapeDtypeStruct((128, 4096), BF16),
            jax.ShapeDtypeStruct((128, 512), BF16),
            jax.ShapeDtypeStruct((128, 512), BF16),
            jax.ShapeDtypeStruct((D, 128), BF16),
            jax.ShapeDtypeStruct((2, D), F32),
            jax.ShapeDtypeStruct((2, D), F32),
        ),
        in_specs=[vm, vm, vm, hbm, hbm],
        out_specs=(hbm, vm, vm, vm, vm, vm),
        scratch_shapes=scratch,
        compiler_params=pltpu.CompilerParams(collective_id=0, has_side_effects=True, vmem_limit_bytes=63 * 2**20),
        name="fused",
    )(ws_k, ws_v, ht, queries, grad_out)


def hand_over(*refs):
    ins, outs, bufs = refs[:6], refs[6:12], refs[12:18]
    sems = refs[18]
    fetch = [pltpu.make_async_copy(ins[i], bufs[i], sems.at[i]) for i in range(6)]
    put = [pltpu.make_async_copy(bufs[i], outs[i], sems.at[6 + i]) for i in range(6)]
    for copy in fetch:
        copy.start()
    for i in range(6):
        fetch[i].wait()
        put[i].start()
    for copy in put:
        copy.wait()


def published(arrays):
    hbm = pl.BlockSpec(memory_space=pl.ANY)
    return pl.pallas_call(
        hand_over,
        out_shape=tuple(jax.ShapeDtypeStruct(a.shape, a.dtype) for a in arrays),
        in_specs=[hbm] * 6,
        out_specs=(hbm,) * 6,
        scratch_shapes=[pltpu.VMEM(a.shape, a.dtype) for a in arrays] + [pltpu.SemaphoreType.DMA((12,))],
        name="hand_over",
    )(*arrays)


def shards(hidden_in, queries, grad_out, key_weight, value_weight):
    dq, gk, gv, git, dwk, dwv = published(fused(key_weight.T, value_weight.T, hidden_in.T, queries, grad_out))
    return dq, gk, gv, git.T, dwk.T, dwv.T


def solution(mesh):
    rows = P(("seqa", "seqb"), None)
    columns = P(None, ("seqa", "seqb"))
    return jax.shard_map(
        shards,
        mesh=mesh,
        in_specs=(rows, rows, rows, columns, columns),
        out_specs=(rows, rows, rows, rows, columns, columns),
        check_vma=False,
    )
```

```python
import jax
import jax.numpy as jnp
from jax import lax
from jax.experimental import pallas as pl
from jax.experimental.pallas import tpu as pltpu
from jax.sharding import PartitionSpec as P

KV_HEADS = 8
HEAD = 64
WIN = 128
D = 2880
LANES = ((0, 384, 640), (1408, 1792, 2176), (640, 1024, 1408), (2176, 2560, 2880))
FIRST = ("x", "y", "x", "y")
FAR = (4, 3, 5, 2, 6, 1, 7)
NT = (((1,), (1,)), ((), ()))
NN = (((1,), (0,)), ((), ()))
MESH = pl.DeviceIdType.MESH
BF16 = jnp.bfloat16
F32 = jnp.float32
FACTOR = HEAD ** (-0.5)
LOG2E = 1.4426950408889634


def coords():
    a = lax.axis_index("seqa")
    b = lax.axis_index("seqb")
    x_lo = a // 8
    y = lax.rem(a // 2, 4)
    core = lax.rem(a, 2)
    x_hi = b // 8
    z = lax.rem(b, 8)
    return x_hi * 2 + x_lo, y, z, core


def at(x, y, z, core):
    return (lax.rem(x, 2) * 8 + y * 2 + core, (x // 2) * 8 + z)


def along(step):
    a = lax.axis_index("seqa")
    b = lax.axis_index("seqb")
    index = lax.rem(a * 16 + b + step + 256, 256)
    return (index // 16, lax.rem(index, 16))


def meet():
    x, y, z, core = coords()
    found = [at(x, y, lax.rem(z + k, 8), core) for k in range(1, 8)]
    found += [at(lax.rem(x + k, 4), y, z, core) for k in (1, 3)]
    found += [at(x, lax.rem(y + k, 4), z, core) for k in (1, 3)]
    found += [at(x, y, z, 1 - core), along(1), along(-1)]
    barrier = pltpu.get_barrier_semaphore()
    for device in found:
        pl.semaphore_signal(barrier, inc=1, device_id=device, device_id_type=MESH)
    pl.semaphore_wait(barrier, len(found))


class Wire:
    def __init__(self, sems):
        self.sems, self.used, self.open = sems, 0, []

    def take(self, count):
        found = [self.sems.at[self.used + i] for i in range(count)]
        self.used += count
        return found

    def send(self, src, dst, device, leaving, landing):
        copy = pltpu.make_async_remote_copy(
            src_ref=src, dst_ref=dst, send_sem=leaving, recv_sem=landing, device_id=device, device_id_type=MESH
        )
        copy.start()
        return copy

    def alone(self, src, dst, device):
        copy = self.send(src, dst, device, *self.take(2))
        self.open.append(copy)
        return copy

    def finish(self):
        for copy in self.open:
            copy.wait_send()


def waiting(ref, sem, device):
    return pltpu.make_async_remote_copy(
        src_ref=ref, dst_ref=ref, send_sem=sem, recv_sem=sem, device_id=device, device_id_type=MESH
    )


def ends(axis):
    x, y, z, core = coords()
    p = x if axis == "x" else y
    plus, minus, opposite = lax.rem(p + 1, 4), lax.rem(p + 3, 4), lax.rem(p + 2, 4)
    if axis == "x":
        return p, plus, minus, opposite, at(plus, y, z, core), at(minus, y, z, core)
    return p, plus, minus, opposite, at(x, plus, z, core), at(x, minus, z, core)


def settle_sends(w, lanes, leaving):
    x, y, z, core = coords()
    lo, hi = lanes[0], lanes[2]
    other = at(x, y, z, 1 - core)
    waiting(w.at[0, 0:3, 0, 0, :, lo:hi], leaving[0], other).wait_send()
    waiting(w.at[:, 0:3, 0, :, :, lo:hi], leaving[1], other).wait_send()


def settle_across(w, lanes, leaving):
    x, y, z, core = coords()
    waiting(w.at[:, :, core, :, :, lanes[0] : lanes[2]], leaving[2], at(x, y, z, 1 - core)).wait_send()


def gather_flow(wire, w, lanes, first, leaving, landing):
    x, y, z, core = coords()
    lo, mid, hi = lanes
    other = at(x, y, z, 1 - core)
    near, lines, over = leaving
    from_minus, from_plus, half_a, half_b, m_own, m_minus, m_rest, p_plus, p_far, p_rest, rel_a, rel_b, home = landing
    p, plus, minus, far, to_plus, to_minus = ends(first)
    q, q_plus, q_minus, q_far, up, down = ends("y" if first == "x" else "x")

    def block(a, b, l0=lo, l1=hi):
        if first == "x":
            return w.at[lax.rem(a, 2), b, core, a // 2, :, l0:l1]
        return w.at[lax.rem(b, 2), a, core, b // 2, :, l0:l1]

    def line(b):
        if first == "x":
            return w.at[:, b, core, :, :, lo:hi]
        return w.at[lax.rem(b, 2), :, core, b // 2, :, lo:hi]

    def put(ref, device, leave, land):
        return wire.send(ref, ref, device, leave, land)

    two = w.at[0, 0, 0, 0:2, :, lo:hi]
    a = put(block(p, q), to_plus, near, from_minus)
    b = put(block(p, q), to_minus, near, from_plus)
    c = put(block(p, q), up, lines, m_own)
    put(block(p, q), down, lines, p_rest)
    put(block(p, q), other, over, home)
    yield
    a.wait_recv()
    d = put(block(minus, q, lo, mid), to_plus, near, half_a)
    e = put(block(minus, q), up, lines, m_minus)
    put(block(minus, q), down, lines, p_rest)
    b.wait_recv()
    f = put(block(plus, q, mid, hi), to_minus, near, half_b)
    g = put(block(plus, q), down, lines, p_plus)
    put(block(plus, q), up, lines, m_rest)
    c.wait_recv()
    put(block(p, q_minus), up, lines, rel_a)
    put(block(minus, q), other, over, home)
    put(block(plus, q), other, over, home)
    yield
    d.wait_recv()
    f.wait_recv()
    h = put(block(far, q), down, lines, p_far)
    put(block(far, q), up, lines, m_rest)
    put(block(far, q), other, over, home)
    e.wait_recv()
    put(block(minus, q_minus), up, lines, rel_a)
    g.wait_recv()
    put(block(plus, q_plus), down, lines, rel_b)
    yield
    h.wait_recv()
    put(block(far, q_plus), down, lines, rel_b)
    waiting(two, m_rest, other).wait_recv()
    put(line(q_minus), other, over, home)
    waiting(two, p_rest, other).wait_recv()
    put(line(q_plus), other, over, home)
    yield
    waiting(two, rel_a, other).wait_recv()
    waiting(two, rel_b, other).wait_recv()
    put(line(q_far), other, over, home)
    yield
    waiting(w.at[:, :, 1 - core, :, :, lo:hi], home, other).wait_recv()
    yield


def reduce_flow(wire, acc, fin, lanes, first, leaving, landing, bufs):
    s1, r1, s0, r0, s2, r2, s3a, r3a, s3b, r3b, s4, r4 = bufs
    lo, mid, hi = lanes
    cut = mid - lo
    near, lines = leaving[0], leaving[1]
    p, plus, minus, far, to_plus, to_minus = ends(first)
    own, up_to, down_to, across, up, down = ends("y" if first == "x" else "x")

    def block(a, b, l0=lo, l1=hi):
        if first == "y":
            return (lax.rem(b, 2), a, b // 2, slice(None), slice(l0, l1))
        return (lax.rem(a, 2), b, a // 2, slice(None), slice(l0, l1))

    some = (down_to, own)
    rest = (across, up_to)
    for i in range(2):
        s1[0, i] = acc[block(far, some[i])].astype(BF16)
        s1[1, i] = acc[block(far, rest[i])].astype(BF16)
    a = wire.send(s1.at[0], r1.at[0], to_plus, lines, landing[0])
    b = wire.send(s1.at[1], r1.at[1], to_minus, lines, landing[1])
    for i in range(2):
        s0[0, i] = acc[block(plus, rest[i])].astype(BF16)
        s0[1, i] = acc[block(minus, some[i])].astype(BF16)
    c = wire.send(s0.at[0], r0.at[0], to_plus, lines, landing[2])
    d = wire.send(s0.at[1], r0.at[1], to_minus, lines, landing[3])
    yield
    a.wait_recv()
    for i in range(2):
        s2[0, i] = (acc[block(plus, some[i])] + r1[0, i].astype(F32)).astype(BF16)
    e = wire.send(s2.at[0], r2.at[0], to_plus, lines, landing[4])
    b.wait_recv()
    for i in range(2):
        s2[1, i] = (acc[block(minus, rest[i])] + r1[1, i].astype(F32)).astype(BF16)
    f = wire.send(s2.at[1], r2.at[1], to_minus, lines, landing[5])
    yield
    c.wait_recv()
    f.wait_recv()
    total = [acc[block(p, rest[i])] + r0[0, i].astype(F32) + r2[1, i].astype(F32) for i in range(2)]
    s3a[...] = total[0][:, :cut].astype(BF16)
    s3b[...] = total[0][:, cut:].astype(BF16)
    a = wire.send(s3a, r3a, up, near, landing[6])
    b = wire.send(s3b, r3b, down, near, landing[7])
    acc[block(p, up_to)] = total[1]
    s4[0, :, cut:] = total[1][:, cut:].astype(BF16)
    d.wait_recv()
    e.wait_recv()
    total = [acc[block(p, some[i])] + r0[1, i].astype(F32) + r2[0, i].astype(F32) for i in range(2)]
    acc[block(p, down_to)] = total[0]
    acc[block(p, own)] = total[1]
    s4[1, :, :cut] = total[0][:, :cut].astype(BF16)
    yield
    a.wait_recv()
    s4[0, :, :cut] = (acc[block(p, up_to, lo, mid)] + r3a[...].astype(F32)).astype(BF16)
    c = wire.send(s4.at[0], r4.at[0], up, near, landing[8])
    b.wait_recv()
    s4[1, :, cut:] = (acc[block(p, down_to, mid, hi)] + r3b[...].astype(F32)).astype(BF16)
    d = wire.send(s4.at[1], r4.at[1], down, near, landing[9])
    yield
    c.wait_recv()
    d.wait_recv()
    fin[:, lo:hi] = acc[block(p, own)] + r4[0].astype(F32) + r4[1].astype(F32)
    yield


def flow_buffers(lanes):
    lo, mid, hi = lanes
    shapes = [(2, 2, 16, hi - lo)] * 6
    shapes += [(16, mid - lo)] * 2 + [(16, hi - mid)] * 2 + [(2, 16, hi - lo)] * 2
    return [pltpu.VMEM(shape, BF16) for shape in shapes]


def step(*flows):
    for flow in flows:
        next(flow)


def kernel(ws_k, ws_v, ht, q_in, g_in, dq, gk, gv, git, dwk, dwv, *scratch):
    (
        zgk, zgv, tk, tv, wk, wv, hto, kt, vt, qv, gvm, qa, ga, pall, ds_s, bias, dqo,
        dko, dvo, dkp, dvp, dkl, dvl, gkt, gvt, gko, gvo, acc_k, acc_v, fin_k, fin_v,
        zsk, zsv, zrk, zrv, zfk, zfv, gkr, gvr, gir,
    ) = scratch[:40]
    bufs = [scratch[40 + 12 * i : 52 + 12 * i] for i in range(8)]
    sems, local_sems = scratch[136:]
    x, y, z, core = coords()
    x_lo, x_hi = lax.rem(x, 2), x // 2
    other = at(x, y, z, 1 - core)
    before, after = along(-1), along(1)
    loads = [
        pltpu.make_async_copy(q_in, qv, local_sems.at[0]),
        pltpu.make_async_copy(g_in, gvm, local_sems.at[1]),
    ]
    for copy in loads:
        copy.start()
    meet()
    wire = Wire(sems)

    k_marks = [(wire.take(3), wire.take(13)) for _ in LANES]
    v_marks = [(wire.take(3), wire.take(13)) for _ in LANES]
    z_marks = [wire.take(2) for _ in range(4)]

    def spread(src, dst, marks):
        for k in FAR:
            wire.send(src, dst.at[z], at(x, y, lax.rem(z + k, 8), core), *marks)

    spread(ws_k, zgk, z_marks[0])
    spread(ws_v, zgv, z_marks[1])
    zgk[z] = ws_k[...]
    zgv[z] = ws_v[...]

    def assemble(marks, zg, rows, w):
        waiting(zg.at[0:7], marks[1], other).wait_recv()
        for i in range(8):
            rows[2 * i : 2 * i + 2] = zg[i].astype(F32)
        w[x_lo, y, core, x_hi] = rows[...].astype(BF16)

    assemble(z_marks[0], zgk, tk, wk)
    k_in = [gather_flow(wire, wk, lanes, axis, *marks) for lanes, axis, marks in zip(LANES, FIRST, k_marks)]
    step(*k_in)
    assemble(z_marks[1], zgv, tv, wv)
    v_in = [gather_flow(wire, wv, lanes, axis, *marks) for lanes, axis, marks in zip(LANES, FIRST, v_marks)]
    step(*k_in)

    first_device = (lax.axis_index("seqa") + lax.axis_index("seqb")) == 0
    s_pos = lax.broadcasted_iota(jnp.int32, (256, 128), 0)
    t_pos = lax.broadcasted_iota(jnp.int32, (256, 128), 1)
    gap = t_pos + 128 - s_pos
    allowed = (gap >= 0) & (gap <= WIN) & (s_pos >= jnp.where(first_device, 128, 0))
    bias[...] = jnp.where(allowed, 0.0, -1e30).astype(F32)
    step(*k_in)
    step(*v_in)
    hc = wire.alone(ht, hto, other)
    for copy in loads:
        copy.wait()

    def stage(j, carry):
        for src, dst in ((qv, qa), (gvm, ga)):
            rows = src[:, pl.ds(pl.multiple_of(512 * j, 512), 512)]
            for h in range(8):
                dst[j, 128 * h : 128 * h + 128] = rows[:, 64 * h : 64 * h + 64]
        return carry

    lax.fori_loop(0, 8, stage, 0)
    step(*k_in)
    step(*v_in)
    step(*k_in)

    def project(w, out, which):
        flat = w[:, :, which].reshape(256, D)
        rows = lax.dot_general(flat, ht[...], NN, preferred_element_type=F32)
        out[:, which, :, 128:256] = rows.astype(BF16).reshape(8, 32, 128)

    def pass_on(arr, a, b):
        return wire.alone(arr.at[a:b, :, :, 128:256], arr.at[a:b, :, :, 0:128], after)

    def pass_back(arr, dst, a, b):
        return wire.alone(arr.at[a:b], dst.at[a:b], before)

    project(wk, kt, core)
    step(*k_in)
    project(wk, kt, 1 - core)
    k_halo = [pass_on(kt, 0, 2), pass_on(kt, 2, 5), pass_on(kt, 5, 8)]
    step(*v_in)

    def forward(j, carry):
        kj = jnp.transpose(kt[j].reshape(64, 256))
        for pair in range(4):
            both = lax.dot_general(kj, qa[j, 256 * pair : 256 * pair + 256], NT, preferred_element_type=F32)
            for h in range(2):
                s = both[:, 128 * h : 128 * h + 128] + bias[...]
                peak = jnp.max(s, axis=0, keepdims=True)
                e = jnp.exp2((s - peak) * (FACTOR * LOG2E))
                p = e * (1.0 / jnp.sum(e, axis=0, keepdims=True))
                col = 256 * pair + 128 * h
                pall[j, :, col : col + 128] = p.astype(BF16)
        grad = jnp.transpose(lax.dot_general(pall[j], ga[j], NN, preferred_element_type=F32))
        dvp[j] = grad[:, 0:128].astype(BF16)
        dvo[j] = grad[:, 128:256]
        return carry

    def backward(j, carry):
        k_t = kt[j].reshape(64, 256)
        vj = jnp.transpose(vt[j].reshape(64, 256))
        for pair in range(4):
            both = lax.dot_general(vj, ga[j, 256 * pair : 256 * pair + 256], NT, preferred_element_type=F32)
            for h in range(2):
                col = 256 * pair + 128 * h
                gp = both[:, 128 * h : 128 * h + 128]
                p = pall[j, :, col : col + 128].astype(F32)
                delta = jnp.sum(p * gp, axis=0, keepdims=True)
                ds_s[:, col : col + 128] = (p * (gp - delta)).astype(BF16)
            turned = lax.dot_general(
                k_t, ds_s[:, 256 * pair : 256 * pair + 256], NN, preferred_element_type=F32
            )
            two = jnp.concatenate([turned[:, 0:128], turned[:, 128:256]], axis=0) * FACTOR
            at_col = pl.multiple_of(512 * j + 128 * pair, 128)
            dqo[:, pl.ds(at_col, 128)] = jnp.transpose(two).astype(BF16)
        grad = jnp.transpose(lax.dot_general(ds_s[...], qa[j], NN, preferred_element_type=F32)) * FACTOR
        dkp[j] = grad[:, 0:128].astype(BF16)
        dko[j] = grad[:, 128:256]
        return carry

    k_halo[0].wait_recv()
    lax.fori_loop(0, 2, forward, 0)
    k_halo[1].wait_recv()
    lax.fori_loop(2, 4, forward, 0)
    dv_halo = [pass_back(dvp, dvl, 0, 4)]
    step(*v_in)
    lax.fori_loop(4, 5, forward, 0)
    k_halo[2].wait_recv()
    lax.fori_loop(5, 7, forward, 0)
    dv_halo.append(pass_back(dvp, dvl, 4, 7))
    step(*v_in)
    lax.fori_loop(7, 8, forward, 0)
    dv_halo.append(pass_back(dvp, dvl, 7, 8))
    project(wv, vt, core)
    step(*v_in)
    project(wv, vt, 1 - core)
    v_halo = [pass_on(vt, 0, 2), pass_on(vt, 2, 5), pass_on(vt, 5, 8)]

    def settle(halo, own, later, total, theirs):
        for copy in halo:
            copy.wait_recv()
        total[...] = (own[...] + later[...].astype(F32)).astype(BF16).reshape(8, 2, 32, 128)
        return wire.alone(total.at[:, 1 - core], theirs, other)

    def token_rows(total):
        return jnp.transpose(total[...].reshape(512, 128).astype(F32)).astype(BF16)

    def reduce_start(total, theirs, w, acc, fin, bufs, marks):
        left = jnp.concatenate([total[:, core].reshape(256, 128), theirs[...].reshape(256, 128)], axis=1)
        flows = []
        for i, lanes in enumerate(LANES):
            lo, hi = lanes[0], lanes[2]
            right = jnp.concatenate([ht[lo:hi], hto[lo:hi]], axis=1)
            part = lax.dot_general(left, right, NT, preferred_element_type=F32)
            acc[:, :, :, :, lo:hi] = part.reshape(2, 4, 2, 16, hi - lo)
            leaving, landing = marks[i]
            settle_sends(w, lanes, leaving)
            settle_across(w, lanes, leaving)
            axis = "y" if FIRST[i] == "x" else "x"
            flows.append(reduce_flow(wire, acc, fin, lanes, axis, leaving, landing, bufs[i]))
            step(flows[-1])
        return flows

    def store(src, dst, i):
        copy = pltpu.make_async_copy(src, dst, local_sems.at[i])
        copy.start()
        stores.append(copy)

    stores = []
    swap_v = settle(dv_halo, dvo, dvl, gvt, gvo)
    gvr[...] = token_rows(gvt)
    store(gvr, gv, 2)
    hc.wait_recv()
    swap_v.wait_recv()
    v_out = reduce_start(gvt, gvo, wk, acc_v, fin_v, bufs[0:4], k_marks)
    v_halo[0].wait_recv()
    lax.fori_loop(0, 2, backward, 0)
    v_halo[1].wait_recv()
    lax.fori_loop(2, 3, backward, 0)
    dk_halo = [pass_back(dkp, dkl, 0, 3)]
    step(*v_out)
    lax.fori_loop(3, 5, backward, 0)
    v_halo[2].wait_recv()
    lax.fori_loop(5, 6, backward, 0)
    dk_halo.append(pass_back(dkp, dkl, 3, 6))
    lax.fori_loop(6, 7, backward, 0)
    dk_halo.append(pass_back(dkp, dkl, 6, 7))
    step(*v_out)
    lax.fori_loop(7, 8, backward, 0)
    dk_halo.append(pass_back(dkp, dkl, 7, 8))
    store(dqo, dq, 3)
    step(*v_out)

    def deal(fin, zf, zs, zr, marks):
        for i in range(8):
            zf[i] = fin[2 * i : 2 * i + 2]
        zs[...] = zf[...].astype(BF16)
        for k in FAR:
            to = lax.rem(z + k, 8)
            wire.send(zs.at[to], zr.at[k - 1], at(x, y, to, core), *marks)

    def collect(marks, zf, zr, out):
        waiting(zr, marks[1], other).wait_recv()
        total = zf[z]
        for k in range(7):
            total = total + zr[k].astype(F32)
        out[...] = total * (32768.0 ** (-0.5))

    swap_k = settle(dk_halo, dko, dkl, gkt, gko)
    gkr[...] = token_rows(gkt)
    store(gkr, gk, 4)
    swap_k.wait_recv()
    k_out = reduce_start(gkt, gko, wv, acc_k, fin_k, bufs[4:8], v_marks)
    step(*v_out)
    deal(fin_v, zfv, zsv, zrv, z_marks[2])
    step(*k_out)
    cols = lax.dot_general(gvr[...], wv[...].reshape(512, D), NN, preferred_element_type=F32)
    cols += lax.dot_general(gkr[...], wk[...].reshape(512, D), NN, preferred_element_type=F32)
    gir[...] = jnp.transpose(cols).astype(BF16)
    store(gir, git, 5)
    step(*k_out)
    collect(z_marks[2], zfv, zrv, dwv)
    step(*k_out)
    step(*k_out)
    deal(fin_k, zfk, zsk, zrk, z_marks[3])
    for copy in stores:
        copy.wait()
    collect(z_marks[3], zfk, zrk, dwk)
    for marks, ref in zip(z_marks, (zgk, zgv, zsv, zsk)):
        waiting(ref.at[0:7], marks[0], other).wait_send()
    for lanes, marks in zip(LANES + LANES, k_marks + v_marks):
        settle_sends(wk, lanes, marks[0])
    wire.finish()


SEMS = 8 * 16 + 8 + 2 * (3 + 3 + 3 + 4 + 2 + 1)


def fused(ws_k, ws_v, ht, queries, grad_out):
    dma = pltpu.SemaphoreType.DMA
    vm = pl.BlockSpec(memory_space=pltpu.VMEM)
    hbm = pl.BlockSpec(memory_space=pl.ANY)
    v = pltpu.VMEM
    scratch = [
        v((8, 2, D), BF16), v((8, 2, D), BF16), v((16, D), F32), v((16, D), F32),
        v((2, 4, 2, 2, 16, D), BF16), v((2, 4, 2, 2, 16, D), BF16), v((D, 128), BF16),
        v((8, 2, 32, 256), BF16), v((8, 2, 32, 256), BF16), v((128, 4096), BF16), v((128, 4096), BF16),
        v((8, 1024, 64), BF16), v((8, 1024, 64), BF16), v((8, 256, 1024), BF16), v((256, 1024), BF16),
        v((256, 128), F32), v((128, 4096), BF16),
        v((8, 64, 128), F32), v((8, 64, 128), F32), v((8, 64, 128), BF16), v((8, 64, 128), BF16),
        v((8, 64, 128), BF16), v((8, 64, 128), BF16), v((8, 2, 32, 128), BF16), v((8, 2, 32, 128), BF16),
        v((8, 32, 128), BF16), v((8, 32, 128), BF16), v((2, 4, 2, 16, D), F32), v((2, 4, 2, 16, D), F32),
        v((16, D), F32), v((16, D), F32),
        v((8, 2, D), BF16), v((8, 2, D), BF16), v((7, 2, D), BF16), v((7, 2, D), BF16),
        v((8, 2, D), F32), v((8, 2, D), F32),
        v((128, 512), BF16), v((128, 512), BF16), v((D, 128), BF16),
        *(buf for lanes in LANES + LANES for buf in flow_buffers(lanes)),
        dma((SEMS,)), dma((6,)),
    ]
    return pl.pallas_call(
        kernel,
        out_shape=(
            jax.ShapeDtypeStruct((128, 4096), BF16),
            jax.ShapeDtypeStruct((128, 512), BF16),
            jax.ShapeDtypeStruct((128, 512), BF16),
            jax.ShapeDtypeStruct((D, 128), BF16),
            jax.ShapeDtypeStruct((2, D), F32),
            jax.ShapeDtypeStruct((2, D), F32),
        ),
        in_specs=[vm, vm, vm, hbm, hbm],
        out_specs=(hbm, hbm, hbm, hbm, vm, vm),
        scratch_shapes=scratch,
        compiler_params=pltpu.CompilerParams(collective_id=0, has_side_effects=True, vmem_limit_bytes=63 * 2**20),
        name="fused",
    )(ws_k, ws_v, ht, queries, grad_out)


def hand_over(*refs):
    ins, outs, bufs = refs[:6], refs[6:12], refs[12:18]
    sems = refs[18]
    fetch = [pltpu.make_async_copy(ins[i], bufs[i], sems.at[i]) for i in range(6)]
    put = [pltpu.make_async_copy(bufs[i], outs[i], sems.at[6 + i]) for i in range(6)]
    for copy in fetch:
        copy.start()
    for i in range(6):
        fetch[i].wait()
        put[i].start()
    for copy in put:
        copy.wait()


def published(arrays):
    hbm = pl.BlockSpec(memory_space=pl.ANY)
    return pl.pallas_call(
        hand_over,
        out_shape=tuple(jax.ShapeDtypeStruct(a.shape, a.dtype) for a in arrays),
        in_specs=[hbm] * 6,
        out_specs=(hbm,) * 6,
        scratch_shapes=[pltpu.VMEM(a.shape, a.dtype) for a in arrays] + [pltpu.SemaphoreType.DMA((12,))],
        name="hand_over",
    )(*arrays)


def shards(hidden_in, queries, grad_out, key_weight, value_weight):
    dq, gk, gv, git, dwk, dwv = published(fused(key_weight.T, value_weight.T, hidden_in.T, queries, grad_out))
    return dq, gk, gv, git.T, dwk.T, dwv.T


def solution(mesh):
    rows = P(("seqa", "seqb"), None)
    columns = P(None, ("seqa", "seqb"))
    return jax.shard_map(
        shards,
        mesh=mesh,
        in_specs=(rows, rows, rows, columns, columns),
        out_specs=(rows, rows, rows, rows, columns, columns),
        check_vma=False,
    )
```

```python
import jax
import jax.numpy as jnp
from jax import lax
from jax.experimental import pallas as pl
from jax.experimental.pallas import tpu as pltpu
from jax.sharding import PartitionSpec as P

KV_HEADS = 8
HEAD = 64
WIN = 128
D = 2880
LANES = ((0, 640), (1408, 2176), (640, 1408), (2176, 2880))
FIRST = ("x", "y", "x", "y")
FAR = (4, 3, 5, 2, 6, 1, 7)
NT = (((1,), (1,)), ((), ()))
NN = (((1,), (0,)), ((), ()))
MESH = pl.DeviceIdType.MESH
BF16 = jnp.bfloat16
F32 = jnp.float32
FACTOR = HEAD ** (-0.5)
LOG2E = 1.4426950408889634


def coords():
    a = lax.axis_index("seqa")
    b = lax.axis_index("seqb")
    x_lo = a // 8
    y = lax.rem(a // 2, 4)
    core = lax.rem(a, 2)
    x_hi = b // 8
    z = lax.rem(b, 8)
    return x_hi * 2 + x_lo, y, z, core


def at(x, y, z, core):
    return (lax.rem(x, 2) * 8 + y * 2 + core, (x // 2) * 8 + z)


def along(step):
    a = lax.axis_index("seqa")
    b = lax.axis_index("seqb")
    index = lax.rem(a * 16 + b + step + 256, 256)
    return (index // 16, lax.rem(index, 16))


def meet():
    x, y, z, core = coords()
    found = [at(x, y, lax.rem(z + k, 8), core) for k in range(1, 8)]
    found += [at(lax.rem(x + k, 4), y, z, core) for k in (1, 2, 3)]
    found += [at(x, lax.rem(y + k, 4), z, core) for k in (1, 2, 3)]
    found += [at(x, y, z, 1 - core), along(1), along(-1)]
    barrier = pltpu.get_barrier_semaphore()
    for device in found:
        pl.semaphore_signal(barrier, inc=1, device_id=device, device_id_type=MESH)
    pl.semaphore_wait(barrier, len(found))


class Wire:
    def __init__(self, sems):
        self.sems, self.used, self.open = sems, 0, []

    def take(self, count):
        found = [self.sems.at[self.used + i] for i in range(count)]
        self.used += count
        return found

    def send(self, src, dst, device, leaving, landing):
        copy = pltpu.make_async_remote_copy(
            src_ref=src, dst_ref=dst, send_sem=leaving, recv_sem=landing, device_id=device, device_id_type=MESH
        )
        copy.start()
        return copy

    def alone(self, src, dst, device):
        copy = self.send(src, dst, device, *self.take(2))
        self.open.append(copy)
        return copy

    def finish(self):
        for copy in self.open:
            copy.wait_send()


def waiting(ref, sem, device):
    return pltpu.make_async_remote_copy(
        src_ref=ref, dst_ref=ref, send_sem=sem, recv_sem=sem, device_id=device, device_id_type=MESH
    )


def ends(axis):
    x, y, z, core = coords()
    p = x if axis == "x" else y
    plus, minus, opposite = lax.rem(p + 1, 4), lax.rem(p + 3, 4), lax.rem(p + 2, 4)
    if axis == "x":
        return p, plus, minus, opposite, [at(q, y, z, core) for q in (plus, minus, opposite)]
    return p, plus, minus, opposite, [at(x, q, z, core) for q in (plus, minus, opposite)]


def settle_sends(w, lanes, leaving):
    x, y, z, core = coords()
    lo, hi = lanes
    other = at(x, y, z, 1 - core)
    waiting(w.at[0, 0:3, 0, 0, :, lo:hi], leaving[0], other).wait_send()
    waiting(w.at[:, 0:3, 0, :, :, lo:hi], leaving[1], other).wait_send()


def settle_across(w, lanes, leaving):
    x, y, z, core = coords()
    waiting(w.at[:, :, core, :, :, lanes[0] : lanes[1]], leaving[2], at(x, y, z, 1 - core)).wait_send()


def gather_flow(wire, w, lanes, first, leaving, landing):
    x, y, z, core = coords()
    lo, hi = lanes
    other = at(x, y, z, 1 - core)
    near, lines, over = leaving
    from_minus, from_plus, from_far, m_own, m_minus, m_rest, p_plus, p_far, p_rest, rel_a, rel_b, home = landing
    p, plus, minus, far, (to_plus, to_minus, to_far) = ends(first)
    q, q_plus, q_minus, q_far, (up, down, _) = ends("y" if first == "x" else "x")

    def block(a, b):
        if first == "x":
            return w.at[lax.rem(a, 2), b, core, a // 2, :, lo:hi]
        return w.at[lax.rem(b, 2), a, core, b // 2, :, lo:hi]

    def line(b):
        if first == "x":
            return w.at[:, b, core, :, :, lo:hi]
        return w.at[lax.rem(b, 2), :, core, b // 2, :, lo:hi]

    def put(ref, device, leave, land):
        return wire.send(ref, ref, device, leave, land)

    two = w.at[0, 0, 0, 0:2, :, lo:hi]
    a = put(block(p, q), to_plus, near, from_minus)
    b = put(block(p, q), to_minus, near, from_plus)
    c = put(block(p, q), to_far, near, from_far)
    yield
    d = put(block(p, q), up, lines, m_own)
    put(block(p, q), down, lines, p_rest)
    put(block(p, q), other, over, home)
    yield
    a.wait_recv()
    e = put(block(minus, q), up, lines, m_minus)
    put(block(minus, q), down, lines, p_rest)
    b.wait_recv()
    f = put(block(plus, q), down, lines, p_plus)
    put(block(plus, q), up, lines, m_rest)
    c.wait_recv()
    g = put(block(far, q), down, lines, p_far)
    put(block(far, q), up, lines, m_rest)
    d.wait_recv()
    put(block(p, q_minus), up, lines, rel_a)
    for near_block in (minus, plus, far):
        put(block(near_block, q), other, over, home)
    yield
    e.wait_recv()
    put(block(minus, q_minus), up, lines, rel_a)
    f.wait_recv()
    put(block(plus, q_plus), down, lines, rel_b)
    g.wait_recv()
    put(block(far, q_plus), down, lines, rel_b)
    waiting(two, m_rest, other).wait_recv()
    put(line(q_minus), other, over, home)
    waiting(two, p_rest, other).wait_recv()
    put(line(q_plus), other, over, home)
    yield
    waiting(two, rel_a, other).wait_recv()
    waiting(two, rel_b, other).wait_recv()
    put(line(q_far), other, over, home)
    yield
    waiting(w.at[:, :, 1 - core, :, :, lo:hi], home, other).wait_recv()
    yield


def reduce_flow(wire, acc, fin, lanes, first, leaving, landing, bufs):
    s1, r1, s0, r0, s2, r2, s3, r3 = bufs
    lo, hi = lanes
    near, lines = leaving[0], leaving[1]
    p, plus, minus, far, (to_plus, to_minus, _) = ends(first)
    own, up_to, down_to, across, (up, down, over) = ends("y" if first == "x" else "x")

    def block(a, b):
        if first == "y":
            return (lax.rem(b, 2), a, b // 2, slice(None), slice(lo, hi))
        return (lax.rem(a, 2), b, a // 2, slice(None), slice(lo, hi))

    some = (down_to, own)
    rest = (across, up_to)
    for i in range(2):
        s1[0, i] = acc[block(far, some[i])].astype(BF16)
        s1[1, i] = acc[block(far, rest[i])].astype(BF16)
    a = wire.send(s1.at[0], r1.at[0], to_plus, lines, landing[0])
    b = wire.send(s1.at[1], r1.at[1], to_minus, lines, landing[1])
    yield
    for i in range(2):
        s0[0, i] = acc[block(plus, rest[i])].astype(BF16)
        s0[1, i] = acc[block(minus, some[i])].astype(BF16)
    c = wire.send(s0.at[0], r0.at[0], to_plus, lines, landing[2])
    d = wire.send(s0.at[1], r0.at[1], to_minus, lines, landing[3])
    yield
    a.wait_recv()
    for i in range(2):
        s2[0, i] = (acc[block(plus, some[i])] + r1[0, i].astype(F32)).astype(BF16)
    e = wire.send(s2.at[0], r2.at[0], to_plus, lines, landing[4])
    b.wait_recv()
    for i in range(2):
        s2[1, i] = (acc[block(minus, rest[i])] + r1[1, i].astype(F32)).astype(BF16)
    f = wire.send(s2.at[1], r2.at[1], to_minus, lines, landing[5])
    yield
    c.wait_recv()
    f.wait_recv()
    for i in range(2):
        s3[i] = (acc[block(p, rest[i])] + r0[0, i].astype(F32) + r2[1, i].astype(F32)).astype(BF16)
    a = wire.send(s3.at[0], r3.at[0], over, near, landing[6])
    b = wire.send(s3.at[1], r3.at[1], up, near, landing[7])
    d.wait_recv()
    e.wait_recv()
    s3[2] = (acc[block(p, down_to)] + r0[1, 0].astype(F32) + r2[0, 0].astype(F32)).astype(BF16)
    c = wire.send(s3.at[2], r3.at[2], down, near, landing[8])
    acc[block(p, own)] = acc[block(p, own)] + r0[1, 1].astype(F32) + r2[0, 1].astype(F32)
    yield
    a.wait_recv()
    b.wait_recv()
    c.wait_recv()
    fin[:, lo:hi] = acc[block(p, own)] + r3[0].astype(F32) + r3[1].astype(F32) + r3[2].astype(F32)
    yield


def flow_buffers(lanes):
    lo, hi = lanes
    shapes = [(2, 2, 16, hi - lo)] * 6 + [(3, 16, hi - lo)] * 2
    return [pltpu.VMEM(shape, BF16) for shape in shapes]


def step(*flows):
    for flow in flows:
        next(flow)


def kernel(ws_k, ws_v, h_in, q_in, g_in, dq, gk, gv, git, dwk, dwv, *scratch):
    (
        zgk, zgv, tk, tv, wk, wv, hto, kt, vt, qv, gvm, qa, ga, pall, ds_s, bias, dqo,
        dko, dvo, dkp, dvp, dkl, dvl, gkt, gvt, gko, gvo, acc_k, acc_v, fin_k, fin_v,
        zsk, zsv, zrk, zrv, zfk, zfv, gkr, gvr, gir, cols_v, ht,
    ) = scratch[:42]
    bufs = [scratch[42 + 8 * i : 50 + 8 * i] for i in range(8)]
    sems, local_sems = scratch[106:]
    x, y, z, core = coords()
    x_lo, x_hi = lax.rem(x, 2), x // 2
    other = at(x, y, z, 1 - core)
    before, after = along(-1), along(1)
    loads = [
        pltpu.make_async_copy(h_in, ht, local_sems.at[6]),
        pltpu.make_async_copy(q_in, qv, local_sems.at[0]),
        pltpu.make_async_copy(g_in, gvm, local_sems.at[1]),
    ]
    for copy in loads:
        copy.start()
    meet()
    wire = Wire(sems)

    k_marks = [(wire.take(3), wire.take(12)) for _ in LANES]
    v_marks = [(wire.take(3), wire.take(12)) for _ in LANES]
    z_marks = [wire.take(2) for _ in range(4)]

    def spread(src, dst, marks):
        for k in FAR:
            wire.send(src, dst.at[z], at(x, y, lax.rem(z + k, 8), core), *marks)

    spread(ws_k, zgk, z_marks[0])
    spread(ws_v, zgv, z_marks[1])
    zgk[z] = ws_k[...]
    zgv[z] = ws_v[...]

    def assemble(marks, zg, rows, w):
        waiting(zg.at[0:7], marks[1], other).wait_recv()
        for i in range(8):
            rows[2 * i : 2 * i + 2] = zg[i].astype(F32)
        w[x_lo, y, core, x_hi] = rows[...].astype(BF16)

    assemble(z_marks[0], zgk, tk, wk)
    k_in = [gather_flow(wire, wk, lanes, axis, *marks) for lanes, axis, marks in zip(LANES, FIRST, k_marks)]
    step(*k_in)
    step(*k_in)
    assemble(z_marks[1], zgv, tv, wv)
    v_in = [gather_flow(wire, wv, lanes, axis, *marks) for lanes, axis, marks in zip(LANES, FIRST, v_marks)]

    first_device = (lax.axis_index("seqa") + lax.axis_index("seqb")) == 0
    s_pos = lax.broadcasted_iota(jnp.int32, (256, 128), 0)
    t_pos = lax.broadcasted_iota(jnp.int32, (256, 128), 1)
    gap = t_pos + 128 - s_pos
    allowed = (gap >= 0) & (gap <= WIN) & (s_pos >= jnp.where(first_device, 128, 0))
    bias[...] = jnp.where(allowed, 0.0, -1e30).astype(F32)
    for copy in loads:
        copy.wait()

    def stage(j, carry):
        for src, dst in ((qv, qa), (gvm, ga)):
            rows = src[:, pl.ds(pl.multiple_of(512 * j, 512), 512)]
            for h in range(8):
                dst[j, 128 * h : 128 * h + 128] = rows[:, 64 * h : 64 * h + 64]
        return carry

    step(*k_in)
    lax.fori_loop(0, 8, stage, 0)
    step(*k_in)
    step(*v_in)
    step(*v_in)
    hc = wire.alone(ht, hto, other)
    step(*k_in)

    def project(w, out, which):
        flat = w[:, :, which].reshape(256, D)
        rows = lax.dot_general(flat, ht[...], NN, preferred_element_type=F32)
        out[:, which, :, 128:256] = rows.astype(BF16).reshape(8, 32, 128)

    def pass_on(arr, a, b):
        return wire.alone(arr.at[a:b, :, :, 128:256], arr.at[a:b, :, :, 0:128], after)

    def pass_back(arr, dst, a, b):
        return wire.alone(arr.at[a:b], dst.at[a:b], before)

    project(wk, kt, core)
    step(*v_in)
    step(*k_in)
    project(wk, kt, 1 - core)
    k_halo = [pass_on(kt, 0, 2), pass_on(kt, 2, 4), pass_on(kt, 4, 8)]

    def forward(j):
        kj = jnp.transpose(kt[j].reshape(64, 256))
        for pair in range(4):
            both = lax.dot_general(kj, qa[j, 256 * pair : 256 * pair + 256], NT, preferred_element_type=F32)
            for h in range(2):
                s = both[:, 128 * h : 128 * h + 128] + bias[...]
                peak = jnp.max(s, axis=0, keepdims=True)
                e = jnp.exp2((s - peak) * (FACTOR * LOG2E))
                p = e * (1.0 / jnp.sum(e, axis=0, keepdims=True))
                col = 256 * pair + 128 * h
                pall[j, :, col : col + 128] = p.astype(BF16)
        grad = jnp.transpose(lax.dot_general(pall[j], ga[j], NN, preferred_element_type=F32))
        dvp[j] = grad[:, 0:128].astype(BF16)
        dvo[j] = grad[:, 128:256]

    def backward(j, ds_s):
        k_t = kt[j].reshape(64, 256)
        vj = jnp.transpose(vt[j].reshape(64, 256))
        for pair in range(4):
            both = lax.dot_general(vj, ga[j, 256 * pair : 256 * pair + 256], NT, preferred_element_type=F32)
            for h in range(2):
                col = 256 * pair + 128 * h
                gp = both[:, 128 * h : 128 * h + 128]
                p = pall[j, :, col : col + 128].astype(F32)
                delta = jnp.sum(p * gp, axis=0, keepdims=True)
                ds_s[:, col : col + 128] = (p * (gp - delta)).astype(BF16)
            turned = lax.dot_general(
                k_t, ds_s[:, 256 * pair : 256 * pair + 256], NN, preferred_element_type=F32
            )
            two = jnp.concatenate([turned[:, 0:128], turned[:, 128:256]], axis=0) * FACTOR
            at_col = pl.multiple_of(512 * j + 128 * pair, 128)
            dqo[:, pl.ds(at_col, 128)] = jnp.transpose(two).astype(BF16)
        grad = jnp.transpose(lax.dot_general(ds_s[...], qa[j], NN, preferred_element_type=F32)) * FACTOR
        dkp[j] = grad[:, 0:128].astype(BF16)
        dko[j] = grad[:, 128:256]

    def forward_two(i):
        forward(2 * i)
        forward(2 * i + 1)

    def backward_two(i):
        backward(2 * i, ds_s.at[0])
        backward(2 * i + 1, ds_s.at[1])

    k_halo[0].wait_recv()
    forward_two(0)
    step(*v_in)
    k_halo[1].wait_recv()
    forward_two(1)
    dv_halo = [pass_back(dvp, dvl, 0, 4)]
    step(*v_in)
    k_halo[2].wait_recv()
    forward_two(2)
    dv_halo.append(pass_back(dvp, dvl, 4, 6))
    project(wv, vt, core)
    step(*v_in)
    project(wv, vt, 1 - core)
    v_halo = [pass_on(vt, 0, 2), pass_on(vt, 2, 4), pass_on(vt, 4, 8)]
    forward_two(3)
    dv_halo.append(pass_back(dvp, dvl, 6, 8))

    def settle(halo, own, later, total, theirs):
        for copy in halo:
            copy.wait_recv()
        total[...] = (own[...] + later[...].astype(F32)).astype(BF16).reshape(8, 2, 32, 128)
        return wire.alone(total.at[:, 1 - core], theirs, other)

    def token_rows(total):
        return jnp.transpose(total[...].reshape(512, 128).astype(F32)).astype(BF16)

    def reduce_start(total, theirs, w, acc, fin, bufs, marks):
        left = jnp.concatenate([total[:, core].reshape(256, 128), theirs[...].reshape(256, 128)], axis=1)
        flows = []
        for i, lanes in enumerate(LANES):
            lo, hi = lanes
            right = jnp.concatenate([ht[lo:hi], hto[lo:hi]], axis=1)
            part = lax.dot_general(left, right, NT, preferred_element_type=F32)
            acc[:, :, :, :, lo:hi] = part.reshape(2, 4, 2, 16, hi - lo)
            leaving, landing = marks[i]
            settle_sends(w, lanes, leaving)
            settle_across(w, lanes, leaving)
            axis = "y" if FIRST[i] == "x" else "x"
            flows.append(reduce_flow(wire, acc, fin, lanes, axis, leaving, landing, bufs[i]))
            step(flows[-1])
        step(*flows)
        return flows

    def store(src, dst, i):
        copy = pltpu.make_async_copy(src, dst, local_sems.at[i])
        copy.start()
        stores.append(copy)

    stores = []
    v_halo[0].wait_recv()
    backward_two(0)
    swap_v = settle(dv_halo, dvo, dvl, gvt, gvo)
    v_halo[1].wait_recv()
    backward_two(1)
    dk_halo = [pass_back(dkp, dkl, 0, 4)]
    hc.wait_recv()
    swap_v.wait_recv()
    v_out = reduce_start(gvt, gvo, wk, acc_v, fin_v, bufs[0:4], k_marks)
    v_halo[2].wait_recv()
    backward_two(2)
    dk_halo.append(pass_back(dkp, dkl, 4, 6))
    gvr[...] = token_rows(gvt)
    store(gvr, gv, 2)
    cols_v[...] = lax.dot_general(gvr[...], wv[...].reshape(512, D), NN, preferred_element_type=F32)
    step(*v_out)
    backward_two(3)
    dk_halo.append(pass_back(dkp, dkl, 6, 8))
    store(dqo, dq, 3)
    step(*v_out)

    def deal(fin, zf, zs, zr, marks):
        for i in range(8):
            zf[i] = fin[2 * i : 2 * i + 2]
        zs[...] = zf[...].astype(BF16)
        for k in FAR:
            to = lax.rem(z + k, 8)
            wire.send(zs.at[to], zr.at[k - 1], at(x, y, to, core), *marks)

    def collect(marks, zf, zr, out):
        waiting(zr, marks[1], other).wait_recv()
        total = zf[z]
        for k in range(7):
            total = total + zr[k].astype(F32)
        out[...] = total * (32768.0 ** (-0.5))

    swap_k = settle(dk_halo, dko, dkl, gkt, gko)
    gkr[...] = token_rows(gkt)
    store(gkr, gk, 4)
    step(*v_out)
    swap_k.wait_recv()
    k_out = reduce_start(gkt, gko, wv, acc_k, fin_k, bufs[4:8], v_marks)
    deal(fin_v, zfv, zsv, zrv, z_marks[2])
    step(*k_out)
    cols = cols_v[...] + lax.dot_general(gkr[...], wk[...].reshape(512, D), NN, preferred_element_type=F32)
    gir[...] = jnp.transpose(cols).astype(BF16)
    store(gir, git, 5)
    step(*k_out)
    collect(z_marks[2], zfv, zrv, dwv)
    step(*k_out)
    deal(fin_k, zfk, zsk, zrk, z_marks[3])
    for copy in stores:
        copy.wait()
    collect(z_marks[3], zfk, zrk, dwk)
    for marks, ref in zip(z_marks, (zgk, zgv, zsv, zsk)):
        waiting(ref.at[0:7], marks[0], other).wait_send()
    for lanes, marks in zip(LANES + LANES, k_marks + v_marks):
        settle_sends(wk, lanes, marks[0])
    wire.finish()


SEMS = 8 * 15 + 8 + 2 * (3 + 3 + 3 + 4 + 2 + 1)


def fused(ws_k, ws_v, ht, queries, grad_out):
    dma = pltpu.SemaphoreType.DMA
    vm = pl.BlockSpec(memory_space=pltpu.VMEM)
    hbm = pl.BlockSpec(memory_space=pl.ANY)
    v = pltpu.VMEM
    scratch = [
        v((8, 2, D), BF16), v((8, 2, D), BF16), v((16, D), F32), v((16, D), F32),
        v((2, 4, 2, 2, 16, D), BF16), v((2, 4, 2, 2, 16, D), BF16), v((D, 128), BF16),
        v((8, 2, 32, 256), BF16), v((8, 2, 32, 256), BF16), v((128, 4096), BF16), v((128, 4096), BF16),
        v((8, 1024, 64), BF16), v((8, 1024, 64), BF16), v((8, 256, 1024), BF16), v((2, 256, 1024), BF16),
        v((256, 128), F32), v((128, 4096), BF16),
        v((8, 64, 128), F32), v((8, 64, 128), F32), v((8, 64, 128), BF16), v((8, 64, 128), BF16),
        v((8, 64, 128), BF16), v((8, 64, 128), BF16), v((8, 2, 32, 128), BF16), v((8, 2, 32, 128), BF16),
        v((8, 32, 128), BF16), v((8, 32, 128), BF16), v((2, 4, 2, 16, D), F32), v((2, 4, 2, 16, D), F32),
        v((16, D), F32), v((16, D), F32),
        v((8, 2, D), BF16), v((8, 2, D), BF16), v((7, 2, D), BF16), v((7, 2, D), BF16),
        v((8, 2, D), F32), v((8, 2, D), F32),
        v((128, 512), BF16), v((128, 512), BF16), v((D, 128), BF16), v((128, D), F32), v((D, 128), BF16),
        *(buf for lanes in LANES + LANES for buf in flow_buffers(lanes)),
        dma((SEMS,)), dma((7,)),
    ]
    return pl.pallas_call(
        kernel,
        out_shape=(
            jax.ShapeDtypeStruct((128, 4096), BF16),
            jax.ShapeDtypeStruct((128, 512), BF16),
            jax.ShapeDtypeStruct((128, 512), BF16),
            jax.ShapeDtypeStruct((D, 128), BF16),
            jax.ShapeDtypeStruct((2, D), F32),
            jax.ShapeDtypeStruct((2, D), F32),
        ),
        in_specs=[vm, vm, hbm, hbm, hbm],
        out_specs=(hbm, hbm, hbm, hbm, vm, vm),
        scratch_shapes=scratch,
        compiler_params=pltpu.CompilerParams(collective_id=0, has_side_effects=True, vmem_limit_bytes=63 * 2**20),
        name="fused",
    )(ws_k, ws_v, ht, queries, grad_out)


PARTS = (4, 1, 1, 4, 1, 1)


def hand_over(*refs):
    ins, outs, bufs, sems = refs[:6], refs[6:12], refs[12:18], refs[18]
    fetch, put = [], []
    for i, parts in enumerate(PARTS):
        rows = ins[i].shape[0] // parts
        for part in range(parts):
            view = pl.ds(rows * part, rows)
            k = len(fetch)
            fetch.append(pltpu.make_async_copy(ins[i].at[view], bufs[i].at[view], sems.at[2 * k]))
            put.append(pltpu.make_async_copy(bufs[i].at[view], outs[i].at[view], sems.at[2 * k + 1]))
    for copy in fetch:
        copy.start()
    for k, copy in enumerate(fetch):
        copy.wait()
        put[k].start()
    for copy in put:
        copy.wait()


def published(arrays):
    hbm = pl.BlockSpec(memory_space=pl.ANY)
    return pl.pallas_call(
        hand_over,
        out_shape=tuple(jax.ShapeDtypeStruct(a.shape, a.dtype) for a in arrays),
        in_specs=[hbm] * 6,
        out_specs=(hbm,) * 6,
        scratch_shapes=[pltpu.VMEM(a.shape, a.dtype) for a in arrays] + [pltpu.SemaphoreType.DMA((2 * sum(PARTS),))],
        name="hand_over",
    )(*arrays)


def shards(hidden_in, queries, grad_out, key_weight, value_weight):
    dq, gk, gv, git, dwk, dwv = published(fused(key_weight.T, value_weight.T, hidden_in.T, queries, grad_out))
    return dq, gk, gv, git.T, dwk.T, dwv.T


def solution(mesh):
    rows = P(("seqa", "seqb"), None)
    columns = P(None, ("seqa", "seqb"))
    return jax.shard_map(
        shards,
        mesh=mesh,
        in_specs=(rows, rows, rows, columns, columns),
        out_specs=(rows, rows, rows, rows, columns, columns),
        check_vma=False,
    )
```

```python
import jax
import jax.numpy as jnp
from jax import lax
from jax.experimental import pallas as pl
from jax.experimental.pallas import tpu as pltpu
from jax.sharding import PartitionSpec as P

KV_HEADS = 8
HEAD = 64
WIN = 128
D = 2880
LANES = ((0, 640), (1408, 2176), (640, 1408), (2176, 2880))
FIRST = ("x", "y", "x", "y")
FAR = (4, 3, 5, 2, 6, 1, 7)
NT = (((1,), (1,)), ((), ()))
NN = (((1,), (0,)), ((), ()))
MESH = pl.DeviceIdType.MESH
BF16 = jnp.bfloat16
F32 = jnp.float32
FACTOR = HEAD ** (-0.5)
LOG2E = 1.4426950408889634


def coords():
    a = lax.axis_index("seqa")
    b = lax.axis_index("seqb")
    x_lo = a // 8
    y = lax.rem(a // 2, 4)
    core = lax.rem(a, 2)
    x_hi = b // 8
    z = lax.rem(b, 8)
    return x_hi * 2 + x_lo, y, z, core


def at(x, y, z, core):
    return (lax.rem(x, 2) * 8 + y * 2 + core, (x // 2) * 8 + z)


def along(step):
    a = lax.axis_index("seqa")
    b = lax.axis_index("seqb")
    index = lax.rem(a * 16 + b + step + 256, 256)
    return (index // 16, lax.rem(index, 16))


def meet():
    x, y, z, core = coords()
    found = [at(x, y, lax.rem(z + k, 8), core) for k in range(1, 8)]
    found += [at(lax.rem(x + k, 4), y, z, core) for k in (1, 2, 3)]
    found += [at(x, lax.rem(y + k, 4), z, core) for k in (1, 2, 3)]
    found += [at(x, y, z, 1 - core), along(1), along(-1)]
    barrier = pltpu.get_barrier_semaphore()
    for device in found:
        pl.semaphore_signal(barrier, inc=1, device_id=device, device_id_type=MESH)
    pl.semaphore_wait(barrier, len(found))


class Wire:
    def __init__(self, sems):
        self.sems, self.used, self.open = sems, 0, []

    def take(self, count):
        found = [self.sems.at[self.used + i] for i in range(count)]
        self.used += count
        return found

    def send(self, src, dst, device, leaving, landing):
        copy = pltpu.make_async_remote_copy(
            src_ref=src, dst_ref=dst, send_sem=leaving, recv_sem=landing, device_id=device, device_id_type=MESH
        )
        copy.start()
        return copy

    def alone(self, src, dst, device):
        copy = self.send(src, dst, device, *self.take(2))
        self.open.append(copy)
        return copy

    def finish(self):
        for copy in self.open:
            copy.wait_send()


def waiting(ref, sem, device):
    return pltpu.make_async_remote_copy(
        src_ref=ref, dst_ref=ref, send_sem=sem, recv_sem=sem, device_id=device, device_id_type=MESH
    )


def ends(axis):
    x, y, z, core = coords()
    p = x if axis == "x" else y
    plus, minus, opposite = lax.rem(p + 1, 4), lax.rem(p + 3, 4), lax.rem(p + 2, 4)
    if axis == "x":
        return p, plus, minus, opposite, [at(q, y, z, core) for q in (plus, minus, opposite)]
    return p, plus, minus, opposite, [at(x, q, z, core) for q in (plus, minus, opposite)]


def settle_sends(w, lanes, leaving):
    x, y, z, core = coords()
    lo, hi = lanes
    other = at(x, y, z, 1 - core)
    waiting(w.at[0, 0:3, 0, 0, :, lo:hi], leaving[0], other).wait_send()
    waiting(w.at[:, 0:3, 0, :, :, lo:hi], leaving[1], other).wait_send()


def settle_across(w, lanes, leaving):
    x, y, z, core = coords()
    waiting(w.at[:, :, core, :, :, lanes[0] : lanes[1]], leaving[2], at(x, y, z, 1 - core)).wait_send()


def gather_flow(wire, w, lanes, first, leaving, landing):
    x, y, z, core = coords()
    lo, hi = lanes
    other = at(x, y, z, 1 - core)
    near, lines, over = leaving
    from_minus, from_plus, from_far, m_own, m_minus, m_rest, p_plus, p_far, p_rest, rel_a, rel_b, home = landing
    p, plus, minus, far, (to_plus, to_minus, to_far) = ends(first)
    q, q_plus, q_minus, q_far, (up, down, _) = ends("y" if first == "x" else "x")

    def block(a, b):
        if first == "x":
            return w.at[lax.rem(a, 2), b, core, a // 2, :, lo:hi]
        return w.at[lax.rem(b, 2), a, core, b // 2, :, lo:hi]

    def line(b):
        if first == "x":
            return w.at[:, b, core, :, :, lo:hi]
        return w.at[lax.rem(b, 2), :, core, b // 2, :, lo:hi]

    def put(ref, device, leave, land):
        return wire.send(ref, ref, device, leave, land)

    two = w.at[0, 0, 0, 0:2, :, lo:hi]
    a = put(block(p, q), to_plus, near, from_minus)
    b = put(block(p, q), to_minus, near, from_plus)
    c = put(block(p, q), to_far, near, from_far)
    yield
    d = put(block(p, q), up, lines, m_own)
    put(block(p, q), down, lines, p_rest)
    put(block(p, q), other, over, home)
    yield
    a.wait_recv()
    e = put(block(minus, q), up, lines, m_minus)
    put(block(minus, q), down, lines, p_rest)
    b.wait_recv()
    f = put(block(plus, q), down, lines, p_plus)
    put(block(plus, q), up, lines, m_rest)
    c.wait_recv()
    g = put(block(far, q), down, lines, p_far)
    put(block(far, q), up, lines, m_rest)
    d.wait_recv()
    put(block(p, q_minus), up, lines, rel_a)
    for near_block in (minus, plus, far):
        put(block(near_block, q), other, over, home)
    yield
    e.wait_recv()
    put(block(minus, q_minus), up, lines, rel_a)
    f.wait_recv()
    put(block(plus, q_plus), down, lines, rel_b)
    g.wait_recv()
    put(block(far, q_plus), down, lines, rel_b)
    waiting(two, m_rest, other).wait_recv()
    put(line(q_minus), other, over, home)
    waiting(two, p_rest, other).wait_recv()
    put(line(q_plus), other, over, home)
    yield
    waiting(two, rel_a, other).wait_recv()
    waiting(two, rel_b, other).wait_recv()
    put(line(q_far), other, over, home)
    yield
    waiting(w.at[:, :, 1 - core, :, :, lo:hi], home, other).wait_recv()
    yield


def reduce_flow(wire, acc, fin, lanes, first, leaving, landing, bufs):
    s1, r1, s0, r0, s2, r2, s3, r3 = bufs
    lo, hi = lanes
    near, lines = leaving[0], leaving[1]
    p, plus, minus, far, (to_plus, to_minus, _) = ends(first)
    own, up_to, down_to, across, (up, down, over) = ends("y" if first == "x" else "x")

    def block(a, b):
        if first == "y":
            return (lax.rem(b, 2), a, b // 2, slice(None), slice(lo, hi))
        return (lax.rem(a, 2), b, a // 2, slice(None), slice(lo, hi))

    some = (down_to, own)
    rest = (across, up_to)
    for i in range(2):
        s1[0, i] = acc[block(far, some[i])].astype(BF16)
        s1[1, i] = acc[block(far, rest[i])].astype(BF16)
    a = wire.send(s1.at[0], r1.at[0], to_plus, lines, landing[0])
    b = wire.send(s1.at[1], r1.at[1], to_minus, lines, landing[1])
    yield
    for i in range(2):
        s0[0, i] = acc[block(plus, rest[i])].astype(BF16)
        s0[1, i] = acc[block(minus, some[i])].astype(BF16)
    c = wire.send(s0.at[0], r0.at[0], to_plus, lines, landing[2])
    d = wire.send(s0.at[1], r0.at[1], to_minus, lines, landing[3])
    yield
    a.wait_recv()
    for i in range(2):
        s2[0, i] = (acc[block(plus, some[i])] + r1[0, i].astype(F32)).astype(BF16)
    e = wire.send(s2.at[0], r2.at[0], to_plus, lines, landing[4])
    b.wait_recv()
    for i in range(2):
        s2[1, i] = (acc[block(minus, rest[i])] + r1[1, i].astype(F32)).astype(BF16)
    f = wire.send(s2.at[1], r2.at[1], to_minus, lines, landing[5])
    yield
    c.wait_recv()
    f.wait_recv()
    for i in range(2):
        s3[i] = (acc[block(p, rest[i])] + r0[0, i].astype(F32) + r2[1, i].astype(F32)).astype(BF16)
    a = wire.send(s3.at[0], r3.at[0], over, near, landing[6])
    b = wire.send(s3.at[1], r3.at[1], up, near, landing[7])
    d.wait_recv()
    e.wait_recv()
    s3[2] = (acc[block(p, down_to)] + r0[1, 0].astype(F32) + r2[0, 0].astype(F32)).astype(BF16)
    c = wire.send(s3.at[2], r3.at[2], down, near, landing[8])
    acc[block(p, own)] = acc[block(p, own)] + r0[1, 1].astype(F32) + r2[0, 1].astype(F32)
    yield
    a.wait_recv()
    b.wait_recv()
    c.wait_recv()
    fin[:, lo:hi] = acc[block(p, own)] + r3[0].astype(F32) + r3[1].astype(F32) + r3[2].astype(F32)
    yield


def flow_buffers(lanes):
    lo, hi = lanes
    shapes = [(2, 2, 16, hi - lo)] * 6 + [(3, 16, hi - lo)] * 2
    return [pltpu.VMEM(shape, BF16) for shape in shapes]


def step(*flows):
    for flow in flows:
        next(flow)


def kernel(ws_k, ws_v, h_in, q_in, g_in, dq, gk, gv, git, dwk, dwv, *scratch):
    (
        zgk, zgv, tk, tv, wk, wv, hto, kt, vt, qv, gvm, qa, ga, pall, ds_s, bias, dqo,
        dko, dvo, dkp, dvp, dkl, dvl, gkt, gvt, gko, gvo, acc_k, acc_v, fin_k, fin_v,
        zsk, zsv, zrk, zrv, zfk, zfv, gkr, gvr, gir, cols_v, ht, dkr, dvr,
    ) = scratch[:44]
    bufs = [scratch[44 + 8 * i : 52 + 8 * i] for i in range(8)]
    sems, local_sems = scratch[108:]
    x, y, z, core = coords()
    x_lo, x_hi = lax.rem(x, 2), x // 2
    other = at(x, y, z, 1 - core)
    before, after = along(-1), along(1)
    loads = [
        pltpu.make_async_copy(h_in, ht, local_sems.at[6]),
        pltpu.make_async_copy(q_in, qv, local_sems.at[0]),
        pltpu.make_async_copy(g_in, gvm, local_sems.at[1]),
    ]
    for copy in loads:
        copy.start()
    meet()
    wire = Wire(sems)

    k_marks = [(wire.take(3), wire.take(12)) for _ in LANES]
    v_marks = [(wire.take(3), wire.take(12)) for _ in LANES]
    z_marks = [wire.take(2) for _ in range(4)]

    def spread(src, dst, marks):
        for k in FAR:
            wire.send(src, dst.at[z], at(x, y, lax.rem(z + k, 8), core), *marks)

    spread(ws_k, zgk, z_marks[0])
    spread(ws_v, zgv, z_marks[1])
    zgk[z] = ws_k[...]
    zgv[z] = ws_v[...]

    def assemble(marks, zg, rows, w):
        waiting(zg.at[0:7], marks[1], other).wait_recv()
        for i in range(8):
            rows[2 * i : 2 * i + 2] = zg[i].astype(F32)
        w[x_lo, y, core, x_hi] = rows[...].astype(BF16)

    assemble(z_marks[0], zgk, tk, wk)
    k_in = [gather_flow(wire, wk, lanes, axis, *marks) for lanes, axis, marks in zip(LANES, FIRST, k_marks)]
    step(*k_in)
    step(*k_in)
    assemble(z_marks[1], zgv, tv, wv)
    v_in = [gather_flow(wire, wv, lanes, axis, *marks) for lanes, axis, marks in zip(LANES, FIRST, v_marks)]

    first_device = (lax.axis_index("seqa") + lax.axis_index("seqb")) == 0
    s_pos = lax.broadcasted_iota(jnp.int32, (256, 128), 0)
    t_pos = lax.broadcasted_iota(jnp.int32, (256, 128), 1)
    gap = t_pos + 128 - s_pos
    allowed = (gap >= 0) & (gap <= WIN) & (s_pos >= jnp.where(first_device, 128, 0))
    bias[...] = jnp.where(allowed, 0.0, -1e30).astype(F32)
    for copy in loads:
        copy.wait()

    def stage(j, carry):
        for src, dst in ((qv, qa), (gvm, ga)):
            rows = src[:, pl.ds(pl.multiple_of(512 * j, 512), 512)]
            for h in range(8):
                dst[j, 128 * h : 128 * h + 128] = rows[:, 64 * h : 64 * h + 64]
        return carry

    step(*k_in)
    lax.fori_loop(0, 8, stage, 0)
    step(*k_in)
    step(*v_in)
    step(*v_in)
    step(*k_in)

    def project(w, out, which):
        flat = w[:, :, which].reshape(256, D)
        rows = lax.dot_general(flat, ht[...], NN, preferred_element_type=F32)
        out[:, which, :, 128:256] = rows.astype(BF16).reshape(8, 32, 128)

    def pass_on(arr, a, b):
        return wire.alone(arr.at[a:b, :, :, 128:256], arr.at[a:b, :, :, 0:128], after)

    def pass_back(arr, dst, a, b):
        return wire.alone(arr.at[a:b], dst.at[a:b], before)

    project(wk, kt, core)
    step(*k_in)
    project(wk, kt, 1 - core)
    k_halo = [pass_on(kt, 0, 2), pass_on(kt, 2, 4)]
    step(*v_in)

    def probabilities(j):
        kj = jnp.transpose(kt[j].reshape(64, 256))
        for pair in range(4):
            both = lax.dot_general(kj, qa[j, 256 * pair : 256 * pair + 256], NT, preferred_element_type=F32)
            for h in range(2):
                s = both[:, 128 * h : 128 * h + 128] + bias[...]
                peak = jnp.max(s, axis=0, keepdims=True)
                e = jnp.exp2((s - peak) * (FACTOR * LOG2E))
                p = e * (1.0 / jnp.sum(e, axis=0, keepdims=True))
                col = 256 * pair + 128 * h
                pall[j, :, col : col + 128] = p.astype(BF16)

    def value_terms(j):
        grad = jnp.transpose(lax.dot_general(pall[j], ga[j], NN, preferred_element_type=F32))
        dvp[j] = grad[:, 0:128].astype(BF16)
        dvo[j] = grad[:, 128:256]

    def backward(j, ds_s):
        k_t = kt[j].reshape(64, 256)
        vj = jnp.transpose(vt[j].reshape(64, 256))
        for pair in range(4):
            both = lax.dot_general(vj, ga[j, 256 * pair : 256 * pair + 256], NT, preferred_element_type=F32)
            for h in range(2):
                col = 256 * pair + 128 * h
                gp = both[:, 128 * h : 128 * h + 128]
                p = pall[j, :, col : col + 128].astype(F32)
                delta = jnp.sum(p * gp, axis=0, keepdims=True)
                ds_s[:, col : col + 128] = (p * (gp - delta)).astype(BF16)
        turned = lax.dot_general(k_t, ds_s[...], NN, preferred_element_type=F32) * FACTOR
        for pair in range(4):
            col = 256 * pair
            two = jnp.concatenate([turned[:, col : col + 128], turned[:, col + 128 : col + 256]], axis=0)
            at_col = pl.multiple_of(512 * j + 128 * pair, 128)
            dqo[:, pl.ds(at_col, 128)] = jnp.transpose(two).astype(BF16)
        grad = jnp.transpose(lax.dot_general(ds_s[...], qa[j], NN, preferred_element_type=F32)) * FACTOR
        dkp[j] = grad[:, 0:128].astype(BF16)
        dko[j] = grad[:, 128:256]

    def forward_two(i):
        probabilities(2 * i)
        probabilities(2 * i + 1)
        value_terms(2 * i)
        value_terms(2 * i + 1)

    def backward_two(i):
        backward(2 * i, ds_s.at[0])
        backward(2 * i + 1, ds_s.at[1])

    k_halo[0].wait_recv()
    k_halo.append(pass_on(kt, 4, 8))
    forward_two(0)
    k_halo[1].wait_recv()
    forward_two(1)
    step(*v_in)
    dv_halo = [pass_back(dvp, dvl, 0, 4)]
    hc = wire.alone(ht, hto, other)
    k_halo[2].wait_recv()
    forward_two(2)
    dv_halo.append(pass_back(dvp, dvl, 4, 6))
    step(*v_in)
    project(wv, vt, core)
    step(*v_in)
    project(wv, vt, 1 - core)
    v_halo = [pass_on(vt, 0, 2)]
    forward_two(3)
    dv_halo.append(pass_back(dvp, dvl, 6, 8))
    v_halo += [pass_on(vt, 2, 4), pass_on(vt, 4, 8)]

    def settle(halo, own, later, total, theirs):
        for copy in halo:
            copy.wait_recv()
        total[...] = (own[...] + later[...].astype(F32)).astype(BF16).reshape(8, 2, 32, 128)
        return wire.alone(total.at[:, 1 - core], theirs, other)

    def token_rows(total):
        return jnp.transpose(total[...].reshape(512, 128).astype(F32)).astype(BF16)

    def reduce_start(total, theirs, w, acc, fin, bufs, marks):
        left = jnp.concatenate([total[:, core].reshape(256, 128), theirs[...].reshape(256, 128)], axis=1)
        flows = []
        for i, lanes in enumerate(LANES):
            lo, hi = lanes
            right = jnp.concatenate([ht[lo:hi], hto[lo:hi]], axis=1)
            part = lax.dot_general(left, right, NT, preferred_element_type=F32)
            acc[:, :, :, :, lo:hi] = part.reshape(2, 4, 2, 16, hi - lo)
            leaving, landing = marks[i]
            settle_sends(w, lanes, leaving)
            settle_across(w, lanes, leaving)
            axis = "y" if FIRST[i] == "x" else "x"
            flows.append(reduce_flow(wire, acc, fin, lanes, axis, leaving, landing, bufs[i]))
            step(flows[-1])
        step(*flows)
        return flows

    def store(src, dst, i):
        copy = pltpu.make_async_copy(src, dst, local_sems.at[i])
        copy.start()
        stores.append(copy)

    stores = []
    v_halo[0].wait_recv()
    backward_two(0)
    v_halo[1].wait_recv()
    backward_two(1)
    dk_halo = [pass_back(dkp, dkl, 0, 4)]
    v_halo[2].wait_recv()
    backward_two(2)
    dk_halo.append(pass_back(dkp, dkl, 4, 6))
    swap_v = settle(dv_halo, dvo, dvl, gvt, gvo)
    gvr[...] = token_rows(gvt)
    store(gvr, gv, 2)
    cols_v[...] = lax.dot_general(gvr[...], wv[...].reshape(512, D), NN, preferred_element_type=F32)
    hc.wait_recv()
    swap_v.wait_recv()
    v_out = reduce_start(gvt, gvo, wk, acc_v, fin_v, bufs[0:4], k_marks)
    backward_two(3)
    dk_halo.append(pass_back(dkp, dkl, 6, 8))
    store(dqo, dq, 3)
    step(*v_out)

    def deal(fin, zf, zs, zr, marks):
        for i in range(8):
            zf[i] = fin[2 * i : 2 * i + 2]
        zs[...] = zf[...].astype(BF16)
        for k in FAR:
            to = lax.rem(z + k, 8)
            wire.send(zs.at[to], zr.at[k - 1], at(x, y, to, core), *marks)

    def collect(marks, zf, zr, held, out, i):
        waiting(zr, marks[1], other).wait_recv()
        total = zf[z]
        for k in range(7):
            total = total + zr[k].astype(F32)
        held[...] = total * (32768.0 ** (-0.5))
        store(held, out, i)

    swap_k = settle(dk_halo, dko, dkl, gkt, gko)
    gkr[...] = token_rows(gkt)
    store(gkr, gk, 4)
    cols = cols_v[...] + lax.dot_general(gkr[...], wk[...].reshape(512, D), NN, preferred_element_type=F32)
    gir[...] = jnp.transpose(cols).astype(BF16)
    store(gir, git, 5)
    step(*v_out)
    swap_k.wait_recv()
    k_out = reduce_start(gkt, gko, wv, acc_k, fin_k, bufs[4:8], v_marks)
    step(*v_out)
    deal(fin_v, zfv, zsv, zrv, z_marks[2])
    step(*k_out)
    step(*k_out)
    collect(z_marks[2], zfv, zrv, dvr, dwv, 7)
    step(*k_out)
    deal(fin_k, zfk, zsk, zrk, z_marks[3])
    collect(z_marks[3], zfk, zrk, dkr, dwk, 8)
    for marks, ref in zip(z_marks, (zgk, zgv, zsv, zsk)):
        waiting(ref.at[0:7], marks[0], other).wait_send()
    for lanes, marks in zip(LANES + LANES, k_marks + v_marks):
        settle_sends(wk, lanes, marks[0])
    wire.finish()
    for copy in stores:
        copy.wait()


SEMS = 8 * 15 + 8 + 2 * (3 + 3 + 3 + 4 + 2 + 1)


def fused(ws_k, ws_v, ht, queries, grad_out):
    dma = pltpu.SemaphoreType.DMA
    vm = pl.BlockSpec(memory_space=pltpu.VMEM)
    hbm = pl.BlockSpec(memory_space=pl.ANY)
    v = pltpu.VMEM
    scratch = [
        v((8, 2, D), BF16), v((8, 2, D), BF16), v((16, D), F32), v((16, D), F32),
        v((2, 4, 2, 2, 16, D), BF16), v((2, 4, 2, 2, 16, D), BF16), v((D, 128), BF16),
        v((8, 2, 32, 256), BF16), v((8, 2, 32, 256), BF16), v((128, 4096), BF16), v((128, 4096), BF16),
        v((8, 1024, 64), BF16), v((8, 1024, 64), BF16), v((8, 256, 1024), BF16), v((2, 256, 1024), BF16),
        v((256, 128), F32), v((128, 4096), BF16),
        v((8, 64, 128), F32), v((8, 64, 128), F32), v((8, 64, 128), BF16), v((8, 64, 128), BF16),
        v((8, 64, 128), BF16), v((8, 64, 128), BF16), v((8, 2, 32, 128), BF16), v((8, 2, 32, 128), BF16),
        v((8, 32, 128), BF16), v((8, 32, 128), BF16), v((2, 4, 2, 16, D), F32), v((2, 4, 2, 16, D), F32),
        v((16, D), F32), v((16, D), F32),
        v((8, 2, D), BF16), v((8, 2, D), BF16), v((7, 2, D), BF16), v((7, 2, D), BF16),
        v((8, 2, D), F32), v((8, 2, D), F32),
        v((128, 512), BF16), v((128, 512), BF16), v((D, 128), BF16), v((128, D), F32), v((D, 128), BF16), v((2, D), F32), v((2, D), F32),
        *(buf for lanes in LANES + LANES for buf in flow_buffers(lanes)),
        dma((SEMS,)), dma((9,)),
    ]
    return pl.pallas_call(
        kernel,
        out_shape=(
            jax.ShapeDtypeStruct((128, 4096), BF16),
            jax.ShapeDtypeStruct((128, 512), BF16),
            jax.ShapeDtypeStruct((128, 512), BF16),
            jax.ShapeDtypeStruct((D, 128), BF16),
            jax.ShapeDtypeStruct((2, D), F32),
            jax.ShapeDtypeStruct((2, D), F32),
        ),
        in_specs=[vm, vm, hbm, hbm, hbm],
        out_specs=(hbm,) * 6,
        scratch_shapes=scratch,
        compiler_params=pltpu.CompilerParams(collective_id=0, has_side_effects=True, vmem_limit_bytes=63 * 2**20),
        name="fused",
    )(ws_k, ws_v, ht, queries, grad_out)


PARTS = (4, 1, 1, 4, 1, 1)


def hand_over(*refs):
    ins, outs, bufs, sems = refs[:6], refs[6:12], refs[12:18], refs[18]
    fetch, put = [], []
    for i, parts in enumerate(PARTS):
        rows = ins[i].shape[0] // parts
        for part in range(parts):
            view = pl.ds(rows * part, rows)
            k = len(fetch)
            fetch.append(pltpu.make_async_copy(ins[i].at[view], bufs[i].at[view], sems.at[2 * k]))
            put.append(pltpu.make_async_copy(bufs[i].at[view], outs[i].at[view], sems.at[2 * k + 1]))
    for copy in fetch:
        copy.start()
    for k, copy in enumerate(fetch):
        copy.wait()
        put[k].start()
    for copy in put:
        copy.wait()


def published(arrays):
    hbm = pl.BlockSpec(memory_space=pl.ANY)
    return pl.pallas_call(
        hand_over,
        out_shape=tuple(jax.ShapeDtypeStruct(a.shape, a.dtype) for a in arrays),
        in_specs=[hbm] * 6,
        out_specs=(hbm,) * 6,
        scratch_shapes=[pltpu.VMEM(a.shape, a.dtype) for a in arrays] + [pltpu.SemaphoreType.DMA((2 * sum(PARTS),))],
        name="hand_over",
    )(*arrays)


def shards(hidden_in, queries, grad_out, key_weight, value_weight):
    dq, gk, gv, git, dwk, dwv = published(fused(key_weight.T, value_weight.T, hidden_in.T, queries, grad_out))
    return dq, gk, gv, git.T, dwk.T, dwv.T


def solution(mesh):
    rows = P(("seqa", "seqb"), None)
    columns = P(None, ("seqa", "seqb"))
    return jax.shard_map(
        shards,
        mesh=mesh,
        in_specs=(rows, rows, rows, columns, columns),
        out_specs=(rows, rows, rows, rows, columns, columns),
        check_vma=False,
    )
```

```python
import jax
import jax.numpy as jnp
from jax import lax
from jax.experimental import pallas as pl
from jax.experimental.pallas import tpu as pltpu
from jax.sharding import PartitionSpec as P

KV_HEADS = 8
HEAD = 64
WIN = 128
D = 2880
LANES = ((0, 640), (1408, 2176), (640, 1408), (2176, 2880))
FIRST = ("x", "y", "x", "y")
FAR = (4, 3, 5, 2, 6, 1, 7)
NT = (((1,), (1,)), ((), ()))
NN = (((1,), (0,)), ((), ()))
MESH = pl.DeviceIdType.MESH
BF16 = jnp.bfloat16
F32 = jnp.float32
FACTOR = HEAD ** (-0.5)
LOG2E = 1.4426950408889634


def coords():
    a = lax.axis_index("seqa")
    b = lax.axis_index("seqb")
    x_lo = a // 8
    y = lax.rem(a // 2, 4)
    core = lax.rem(a, 2)
    x_hi = b // 8
    z = lax.rem(b, 8)
    return x_hi * 2 + x_lo, y, z, core


def at(x, y, z, core):
    return (lax.rem(x, 2) * 8 + y * 2 + core, (x // 2) * 8 + z)


def along(step):
    a = lax.axis_index("seqa")
    b = lax.axis_index("seqb")
    index = lax.rem(a * 16 + b + step + 256, 256)
    return (index // 16, lax.rem(index, 16))


def meet():
    x, y, z, core = coords()
    found = [at(x, y, lax.rem(z + k, 8), core) for k in range(1, 8)]
    found += [at(lax.rem(x + k, 4), y, z, core) for k in (1, 2, 3)]
    found += [at(x, lax.rem(y + k, 4), z, core) for k in (1, 2, 3)]
    found += [at(x, y, z, 1 - core), along(1), along(-1)]
    barrier = pltpu.get_barrier_semaphore()
    for device in found:
        pl.semaphore_signal(barrier, inc=1, device_id=device, device_id_type=MESH)
    pl.semaphore_wait(barrier, len(found))


class Wire:
    def __init__(self, sems):
        self.sems, self.used, self.open = sems, 0, []

    def take(self, count):
        found = [self.sems.at[self.used + i] for i in range(count)]
        self.used += count
        return found

    def send(self, src, dst, device, leaving, landing):
        copy = pltpu.make_async_remote_copy(
            src_ref=src, dst_ref=dst, send_sem=leaving, recv_sem=landing, device_id=device, device_id_type=MESH
        )
        copy.start()
        return copy

    def alone(self, src, dst, device):
        copy = self.send(src, dst, device, *self.take(2))
        self.open.append(copy)
        return copy

    def finish(self):
        for copy in self.open:
            copy.wait_send()


def waiting(ref, sem, device):
    return pltpu.make_async_remote_copy(
        src_ref=ref, dst_ref=ref, send_sem=sem, recv_sem=sem, device_id=device, device_id_type=MESH
    )


def ends(axis):
    x, y, z, core = coords()
    p = x if axis == "x" else y
    plus, minus, opposite = lax.rem(p + 1, 4), lax.rem(p + 3, 4), lax.rem(p + 2, 4)
    if axis == "x":
        return p, plus, minus, opposite, [at(q, y, z, core) for q in (plus, minus, opposite)]
    return p, plus, minus, opposite, [at(x, q, z, core) for q in (plus, minus, opposite)]


def settle_sends(w, lanes, leaving):
    x, y, z, core = coords()
    lo, hi = lanes
    other = at(x, y, z, 1 - core)
    waiting(w.at[0, 0:3, 0, 0, :, lo:hi], leaving[0], other).wait_send()
    waiting(w.at[:, 0:3, 0, :, :, lo:hi], leaving[1], other).wait_send()


def settle_across(w, lanes, leaving):
    x, y, z, core = coords()
    waiting(w.at[:, :, core, :, :, lanes[0] : lanes[1]], leaving[2], at(x, y, z, 1 - core)).wait_send()


def gather_flow(wire, w, lanes, first, leaving, landing):
    x, y, z, core = coords()
    lo, hi = lanes
    other = at(x, y, z, 1 - core)
    near, lines, over = leaving
    from_minus, from_plus, from_far, m_own, m_minus, m_rest, p_plus, p_far, p_rest, rel_a, rel_b, home = landing
    p, plus, minus, far, (to_plus, to_minus, to_far) = ends(first)
    q, q_plus, q_minus, q_far, (up, down, _) = ends("y" if first == "x" else "x")

    def block(a, b):
        if first == "x":
            return w.at[lax.rem(a, 2), b, core, a // 2, :, lo:hi]
        return w.at[lax.rem(b, 2), a, core, b // 2, :, lo:hi]

    def line(b):
        if first == "x":
            return w.at[:, b, core, :, :, lo:hi]
        return w.at[lax.rem(b, 2), :, core, b // 2, :, lo:hi]

    def put(ref, device, leave, land):
        return wire.send(ref, ref, device, leave, land)

    two = w.at[0, 0, 0, 0:2, :, lo:hi]
    a = put(block(p, q), to_plus, near, from_minus)
    b = put(block(p, q), to_minus, near, from_plus)
    c = put(block(p, q), to_far, near, from_far)
    yield
    d = put(block(p, q), up, lines, m_own)
    put(block(p, q), down, lines, p_rest)
    put(block(p, q), other, over, home)
    yield
    a.wait_recv()
    e = put(block(minus, q), up, lines, m_minus)
    put(block(minus, q), down, lines, p_rest)
    b.wait_recv()
    f = put(block(plus, q), down, lines, p_plus)
    put(block(plus, q), up, lines, m_rest)
    c.wait_recv()
    g = put(block(far, q), down, lines, p_far)
    put(block(far, q), up, lines, m_rest)
    d.wait_recv()
    put(block(p, q_minus), up, lines, rel_a)
    for near_block in (minus, plus, far):
        put(block(near_block, q), other, over, home)
    yield
    e.wait_recv()
    put(block(minus, q_minus), up, lines, rel_a)
    f.wait_recv()
    put(block(plus, q_plus), down, lines, rel_b)
    g.wait_recv()
    put(block(far, q_plus), down, lines, rel_b)
    waiting(two, m_rest, other).wait_recv()
    put(line(q_minus), other, over, home)
    waiting(two, p_rest, other).wait_recv()
    put(line(q_plus), other, over, home)
    yield
    waiting(two, rel_a, other).wait_recv()
    waiting(two, rel_b, other).wait_recv()
    put(line(q_far), other, over, home)
    yield
    waiting(w.at[:, :, 1 - core, :, :, lo:hi], home, other).wait_recv()
    yield


def reduce_flow(wire, acc, fin, lanes, first, leaving, landing, bufs):
    s1, r1, s0, r0, s2, r2, s3, r3 = bufs
    lo, hi = lanes
    near, lines = leaving[0], leaving[1]
    p, plus, minus, far, (to_plus, to_minus, _) = ends(first)
    own, up_to, down_to, across, (up, down, over) = ends("y" if first == "x" else "x")

    def block(a, b):
        if first == "y":
            return (lax.rem(b, 2), a, b // 2, slice(None), slice(lo, hi))
        return (lax.rem(a, 2), b, a // 2, slice(None), slice(lo, hi))

    some = (down_to, own)
    rest = (across, up_to)
    for i in range(2):
        s1[0, i] = acc[block(far, some[i])].astype(BF16)
        s1[1, i] = acc[block(far, rest[i])].astype(BF16)
    a = wire.send(s1.at[0], r1.at[0], to_plus, lines, landing[0])
    b = wire.send(s1.at[1], r1.at[1], to_minus, lines, landing[1])
    yield
    for i in range(2):
        s0[0, i] = acc[block(plus, rest[i])].astype(BF16)
        s0[1, i] = acc[block(minus, some[i])].astype(BF16)
    c = wire.send(s0.at[0], r0.at[0], to_plus, lines, landing[2])
    d = wire.send(s0.at[1], r0.at[1], to_minus, lines, landing[3])
    yield
    a.wait_recv()
    for i in range(2):
        s2[0, i] = (acc[block(plus, some[i])] + r1[0, i].astype(F32)).astype(BF16)
    e = wire.send(s2.at[0], r2.at[0], to_plus, lines, landing[4])
    b.wait_recv()
    for i in range(2):
        s2[1, i] = (acc[block(minus, rest[i])] + r1[1, i].astype(F32)).astype(BF16)
    f = wire.send(s2.at[1], r2.at[1], to_minus, lines, landing[5])
    yield
    c.wait_recv()
    f.wait_recv()
    for i in range(2):
        s3[i] = (acc[block(p, rest[i])] + r0[0, i].astype(F32) + r2[1, i].astype(F32)).astype(BF16)
    a = wire.send(s3.at[0], r3.at[0], over, near, landing[6])
    b = wire.send(s3.at[1], r3.at[1], up, near, landing[7])
    d.wait_recv()
    e.wait_recv()
    s3[2] = (acc[block(p, down_to)] + r0[1, 0].astype(F32) + r2[0, 0].astype(F32)).astype(BF16)
    c = wire.send(s3.at[2], r3.at[2], down, near, landing[8])
    acc[block(p, own)] = acc[block(p, own)] + r0[1, 1].astype(F32) + r2[0, 1].astype(F32)
    yield
    a.wait_recv()
    b.wait_recv()
    c.wait_recv()
    fin[:, lo:hi] = acc[block(p, own)] + r3[0].astype(F32) + r3[1].astype(F32) + r3[2].astype(F32)
    yield


def flow_buffers(lanes):
    lo, hi = lanes
    shapes = [(2, 2, 16, hi - lo)] * 6 + [(3, 16, hi - lo)] * 2
    return [pltpu.VMEM(shape, BF16) for shape in shapes]


def step(*flows):
    for flow in flows:
        next(flow)


def kernel(ws_k, ws_v, h_in, q_in, g_in, dq, gk, gv, git, dwk, dwv, *scratch):
    (
        zgk, zgv, tk, tv, wk, wv, hto, kt, vt, qv, gvm, qa, ga, pall, ds_s, bias, dqo,
        dko, dvo, dkp, dvp, dkl, dvl, gkt, gvt, gko, gvo, acc_k, acc_v, fin_k, fin_v,
        zsk, zsv, zrk, zrv, zfk, zfv, gkr, gvr, gir, cols_v, ht, dkr, dvr,
    ) = scratch[:44]
    bufs = [scratch[44 + 8 * i : 52 + 8 * i] for i in range(8)]
    sems, local_sems = scratch[108:]
    x, y, z, core = coords()
    x_lo, x_hi = lax.rem(x, 2), x // 2
    other = at(x, y, z, 1 - core)
    before, after = along(-1), along(1)
    loads = [
        pltpu.make_async_copy(h_in, ht, local_sems.at[6]),
        pltpu.make_async_copy(q_in, qv, local_sems.at[0]),
        pltpu.make_async_copy(g_in, gvm, local_sems.at[1]),
    ]
    for copy in loads:
        copy.start()
    meet()
    wire = Wire(sems)

    k_marks = [(wire.take(3), wire.take(12)) for _ in LANES]
    v_marks = [(wire.take(3), wire.take(12)) for _ in LANES]
    z_marks = [wire.take(2) for _ in range(4)]

    def spread(src, dst, marks):
        for k in FAR:
            wire.send(src, dst.at[z], at(x, y, lax.rem(z + k, 8), core), *marks)

    spread(ws_k, zgk, z_marks[0])
    spread(ws_v, zgv, z_marks[1])
    zgk[z] = ws_k[...]
    zgv[z] = ws_v[...]

    def assemble(marks, zg, rows, w):
        waiting(zg.at[0:7], marks[1], other).wait_recv()
        for i in range(8):
            rows[2 * i : 2 * i + 2] = zg[i].astype(F32)
        w[x_lo, y, core, x_hi] = rows[...].astype(BF16)

    assemble(z_marks[0], zgk, tk, wk)
    k_in = [gather_flow(wire, wk, lanes, axis, *marks) for lanes, axis, marks in zip(LANES, FIRST, k_marks)]
    step(*k_in)
    step(*k_in)
    assemble(z_marks[1], zgv, tv, wv)
    v_in = [gather_flow(wire, wv, lanes, axis, *marks) for lanes, axis, marks in zip(LANES, FIRST, v_marks)]

    first_device = (lax.axis_index("seqa") + lax.axis_index("seqb")) == 0
    s_pos = lax.broadcasted_iota(jnp.int32, (256, 128), 0)
    t_pos = lax.broadcasted_iota(jnp.int32, (256, 128), 1)
    gap = t_pos + 128 - s_pos
    allowed = (gap >= 0) & (gap <= WIN) & (s_pos >= jnp.where(first_device, 128, 0))
    bias[...] = jnp.where(allowed, 0.0, -1e30).astype(F32)
    for copy in loads:
        copy.wait()

    def stage(j, carry):
        for src, dst in ((qv, qa), (gvm, ga)):
            rows = src[:, pl.ds(pl.multiple_of(512 * j, 512), 512)]
            for h in range(8):
                dst[j, 128 * h : 128 * h + 128] = rows[:, 64 * h : 64 * h + 64]
        return carry

    step(*k_in)
    lax.fori_loop(0, 8, stage, 0)
    step(*k_in)
    step(*v_in)
    step(*v_in)
    step(*k_in)

    def project(w, out, which):
        flat = w[:, :, which].reshape(256, D)
        rows = lax.dot_general(flat, ht[...], NN, preferred_element_type=F32)
        out[:, which, :, 128:256] = rows.astype(BF16).reshape(8, 32, 128)

    def pass_on(arr, a, b):
        return wire.alone(arr.at[a:b, :, :, 128:256], arr.at[a:b, :, :, 0:128], after)

    def pass_back(arr, dst, a, b):
        return wire.alone(arr.at[a:b], dst.at[a:b], before)

    project(wk, kt, core)
    step(*k_in)
    project(wk, kt, 1 - core)
    k_halo = [pass_on(kt, 0, 2), pass_on(kt, 2, 4)]
    step(*v_in)

    def probabilities(j):
        kj = jnp.transpose(kt[j].reshape(64, 256))
        for pair in range(4):
            both = lax.dot_general(kj, qa[j, 256 * pair : 256 * pair + 256], NT, preferred_element_type=F32)
            for h in range(2):
                s = both[:, 128 * h : 128 * h + 128] + bias[...]
                peak = jnp.max(s, axis=0, keepdims=True)
                e = jnp.exp2((s - peak) * (FACTOR * LOG2E))
                p = e * (1.0 / jnp.sum(e, axis=0, keepdims=True))
                col = 256 * pair + 128 * h
                pall[j, :, col : col + 128] = p.astype(BF16)

    def value_terms(j):
        grad = jnp.transpose(lax.dot_general(pall[j], ga[j], NN, preferred_element_type=F32))
        dvp[j] = grad[:, 0:128].astype(BF16)
        dvo[j] = grad[:, 128:256]

    def backward(j, ds_s):
        k_t = kt[j].reshape(64, 256)
        vj = jnp.transpose(vt[j].reshape(64, 256))
        for pair in range(4):
            both = lax.dot_general(vj, ga[j, 256 * pair : 256 * pair + 256], NT, preferred_element_type=F32)
            for h in range(2):
                col = 256 * pair + 128 * h
                gp = both[:, 128 * h : 128 * h + 128]
                p = pall[j, :, col : col + 128].astype(F32)
                delta = jnp.sum(p * gp, axis=0, keepdims=True)
                ds_s[:, col : col + 128] = (p * (gp - delta)).astype(BF16)
        turned = lax.dot_general(k_t, ds_s[...], NN, preferred_element_type=F32) * FACTOR
        for pair in range(4):
            col = 256 * pair
            two = jnp.concatenate([turned[:, col : col + 128], turned[:, col + 128 : col + 256]], axis=0)
            at_col = pl.multiple_of(512 * j + 128 * pair, 128)
            dqo[:, pl.ds(at_col, 128)] = jnp.transpose(two).astype(BF16)
        grad = jnp.transpose(lax.dot_general(ds_s[...], qa[j], NN, preferred_element_type=F32)) * FACTOR
        dkp[j] = grad[:, 0:128].astype(BF16)
        dko[j] = grad[:, 128:256]

    def forward_two(i):
        probabilities(2 * i)
        probabilities(2 * i + 1)
        value_terms(2 * i)
        value_terms(2 * i + 1)

    def backward_two(i):
        backward(2 * i, ds_s.at[0])
        backward(2 * i + 1, ds_s.at[1])

    k_halo[0].wait_recv()
    k_halo.append(pass_on(kt, 4, 8))
    forward_two(0)
    k_halo[1].wait_recv()
    forward_two(1)
    step(*v_in)
    dv_halo = [pass_back(dvp, dvl, 0, 4)]
    hc = wire.alone(ht, hto, other)
    k_halo[2].wait_recv()
    forward_two(2)
    dv_halo.append(pass_back(dvp, dvl, 4, 6))
    step(*v_in)
    project(wv, vt, core)
    step(*v_in)
    project(wv, vt, 1 - core)
    v_halo = [pass_on(vt, 0, 2)]
    forward_two(3)
    dv_halo.append(pass_back(dvp, dvl, 6, 8))
    v_halo += [pass_on(vt, 2, 4), pass_on(vt, 4, 8)]

    def settle(halo, own, later, total, theirs):
        for copy in halo:
            copy.wait_recv()
        total[...] = (own[...] + later[...].astype(F32)).astype(BF16).reshape(8, 2, 32, 128)
        return wire.alone(total.at[:, 1 - core], theirs, other)

    def token_rows(total):
        return jnp.transpose(total[...].reshape(512, 128).astype(F32)).astype(BF16)

    def reduce_start(total, theirs, w, acc, fin, bufs, marks):
        left = jnp.concatenate([total[:, core].reshape(256, 128), theirs[...].reshape(256, 128)], axis=1)
        flows = []
        for i, lanes in enumerate(LANES):
            lo, hi = lanes
            right = jnp.concatenate([ht[lo:hi], hto[lo:hi]], axis=1)
            part = lax.dot_general(left, right, NT, preferred_element_type=F32)
            acc[:, :, :, :, lo:hi] = part.reshape(2, 4, 2, 16, hi - lo)
            leaving, landing = marks[i]
            settle_sends(w, lanes, leaving)
            settle_across(w, lanes, leaving)
            axis = "y" if FIRST[i] == "x" else "x"
            flows.append(reduce_flow(wire, acc, fin, lanes, axis, leaving, landing, bufs[i]))
            step(flows[-1])
        return flows

    def store(src, dst, i):
        copy = pltpu.make_async_copy(src, dst, local_sems.at[i])
        copy.start()
        stores.append(copy)

    stores = []
    v_halo[0].wait_recv()
    backward_two(0)
    v_halo[1].wait_recv()
    backward_two(1)
    dk_halo = [pass_back(dkp, dkl, 0, 4)]
    v_halo[2].wait_recv()
    backward_two(2)
    dk_halo.append(pass_back(dkp, dkl, 4, 6))
    swap_v = settle(dv_halo, dvo, dvl, gvt, gvo)
    gvr[...] = token_rows(gvt)
    store(gvr, gv, 2)
    cols_v[...] = lax.dot_general(gvr[...], wv[...].reshape(512, D), NN, preferred_element_type=F32)
    hc.wait_recv()
    swap_v.wait_recv()
    v_out = reduce_start(gvt, gvo, wk, acc_v, fin_v, bufs[0:4], k_marks)
    backward_two(3)
    dk_halo.append(pass_back(dkp, dkl, 6, 8))
    step(*v_out)
    step(*v_out)
    store(dqo, dq, 3)

    def deal(fin, zf, zs, zr, marks):
        for i in range(8):
            zf[i] = fin[2 * i : 2 * i + 2]
        zs[...] = zf[...].astype(BF16)
        for k in FAR:
            to = lax.rem(z + k, 8)
            wire.send(zs.at[to], zr.at[k - 1], at(x, y, to, core), *marks)

    def collect(marks, zf, zr, held, out, i):
        waiting(zr, marks[1], other).wait_recv()
        total = zf[z]
        for k in range(7):
            total = total + zr[k].astype(F32)
        held[...] = total * (32768.0 ** (-0.5))
        store(held, out, i)

    swap_k = settle(dk_halo, dko, dkl, gkt, gko)
    gkr[...] = token_rows(gkt)
    store(gkr, gk, 4)
    cols = cols_v[...] + lax.dot_general(gkr[...], wk[...].reshape(512, D), NN, preferred_element_type=F32)
    gir[...] = jnp.transpose(cols).astype(BF16)
    store(gir, git, 5)
    step(*v_out)
    swap_k.wait_recv()
    k_out = reduce_start(gkt, gko, wv, acc_k, fin_k, bufs[4:8], v_marks)
    step(*k_out)
    step(*v_out)
    deal(fin_v, zfv, zsv, zrv, z_marks[2])
    step(*k_out)
    step(*k_out)
    collect(z_marks[2], zfv, zrv, dvr, dwv, 7)
    step(*k_out)
    deal(fin_k, zfk, zsk, zrk, z_marks[3])
    collect(z_marks[3], zfk, zrk, dkr, dwk, 8)
    for marks, ref in zip(z_marks, (zgk, zgv, zsv, zsk)):
        waiting(ref.at[0:7], marks[0], other).wait_send()
    for lanes, marks in zip(LANES + LANES, k_marks + v_marks):
        settle_sends(wk, lanes, marks[0])
    wire.finish()
    for copy in stores:
        copy.wait()


SEMS = 8 * 15 + 8 + 2 * (3 + 3 + 3 + 4 + 2 + 1)


def fused(ws_k, ws_v, ht, queries, grad_out):
    dma = pltpu.SemaphoreType.DMA
    vm = pl.BlockSpec(memory_space=pltpu.VMEM)
    hbm = pl.BlockSpec(memory_space=pl.ANY)
    v = pltpu.VMEM
    scratch = [
        v((8, 2, D), BF16), v((8, 2, D), BF16), v((16, D), F32), v((16, D), F32),
        v((2, 4, 2, 2, 16, D), BF16), v((2, 4, 2, 2, 16, D), BF16), v((D, 128), BF16),
        v((8, 2, 32, 256), BF16), v((8, 2, 32, 256), BF16), v((128, 4096), BF16), v((128, 4096), BF16),
        v((8, 1024, 64), BF16), v((8, 1024, 64), BF16), v((8, 256, 1024), BF16), v((2, 256, 1024), BF16),
        v((256, 128), F32), v((128, 4096), BF16),
        v((8, 64, 128), F32), v((8, 64, 128), F32), v((8, 64, 128), BF16), v((8, 64, 128), BF16),
        v((8, 64, 128), BF16), v((8, 64, 128), BF16), v((8, 2, 32, 128), BF16), v((8, 2, 32, 128), BF16),
        v((8, 32, 128), BF16), v((8, 32, 128), BF16), v((2, 4, 2, 16, D), F32), v((2, 4, 2, 16, D), F32),
        v((16, D), F32), v((16, D), F32),
        v((8, 2, D), BF16), v((8, 2, D), BF16), v((7, 2, D), BF16), v((7, 2, D), BF16),
        v((8, 2, D), F32), v((8, 2, D), F32),
        v((128, 512), BF16), v((128, 512), BF16), v((D, 128), BF16), v((128, D), F32), v((D, 128), BF16), v((2, D), F32), v((2, D), F32),
        *(buf for lanes in LANES + LANES for buf in flow_buffers(lanes)),
        dma((SEMS,)), dma((9,)),
    ]
    return pl.pallas_call(
        kernel,
        out_shape=(
            jax.ShapeDtypeStruct((128, 4096), BF16),
            jax.ShapeDtypeStruct((128, 512), BF16),
            jax.ShapeDtypeStruct((128, 512), BF16),
            jax.ShapeDtypeStruct((D, 128), BF16),
            jax.ShapeDtypeStruct((2, D), F32),
            jax.ShapeDtypeStruct((2, D), F32),
        ),
        in_specs=[vm, vm, hbm, hbm, hbm],
        out_specs=(hbm,) * 6,
        scratch_shapes=scratch,
        compiler_params=pltpu.CompilerParams(collective_id=0, has_side_effects=True, vmem_limit_bytes=63 * 2**20),
        name="fused",
    )(ws_k, ws_v, ht, queries, grad_out)


PARTS = (4, 1, 1, 4, 1, 1)


def hand_over(*refs):
    ins, outs, bufs, sems = refs[:6], refs[6:12], refs[12:18], refs[18]
    fetch, put = [], []
    for i, parts in enumerate(PARTS):
        rows = ins[i].shape[0] // parts
        for part in range(parts):
            view = pl.ds(rows * part, rows)
            k = len(fetch)
            fetch.append(pltpu.make_async_copy(ins[i].at[view], bufs[i].at[view], sems.at[2 * k]))
            put.append(pltpu.make_async_copy(bufs[i].at[view], outs[i].at[view], sems.at[2 * k + 1]))
    for copy in fetch:
        copy.start()
    for k, copy in enumerate(fetch):
        copy.wait()
        put[k].start()
    for copy in put:
        copy.wait()


def published(arrays):
    hbm = pl.BlockSpec(memory_space=pl.ANY)
    return pl.pallas_call(
        hand_over,
        out_shape=tuple(jax.ShapeDtypeStruct(a.shape, a.dtype) for a in arrays),
        in_specs=[hbm] * 6,
        out_specs=(hbm,) * 6,
        scratch_shapes=[pltpu.VMEM(a.shape, a.dtype) for a in arrays] + [pltpu.SemaphoreType.DMA((2 * sum(PARTS),))],
        name="hand_over",
    )(*arrays)


def shards(hidden_in, queries, grad_out, key_weight, value_weight):
    dq, gk, gv, git, dwk, dwv = published(fused(key_weight.T, value_weight.T, hidden_in.T, queries, grad_out))
    return dq, gk, gv, git.T, dwk.T, dwv.T


def solution(mesh):
    rows = P(("seqa", "seqb"), None)
    columns = P(None, ("seqa", "seqb"))
    return jax.shard_map(
        shards,
        mesh=mesh,
        in_specs=(rows, rows, rows, columns, columns),
        out_specs=(rows, rows, rows, rows, columns, columns),
        check_vma=False,
    )
```

```python
import jax
import jax.numpy as jnp
from jax import lax
from jax.experimental import pallas as pl
from jax.experimental.pallas import tpu as pltpu
from jax.sharding import PartitionSpec as P

KV_HEADS = 8
HEAD = 64
WIN = 128
D = 2880
LANES = ((0, 640), (1408, 2176), (640, 1408), (2176, 2880))
FIRST = ("x", "y", "x", "y")
FAR = (4, 3, 5, 2, 6, 1, 7)
NT = (((1,), (1,)), ((), ()))
NN = (((1,), (0,)), ((), ()))
MESH = pl.DeviceIdType.MESH
BF16 = jnp.bfloat16
F32 = jnp.float32
FACTOR = HEAD ** (-0.5)
LOG2E = 1.4426950408889634


def coords():
    a = lax.axis_index("seqa")
    b = lax.axis_index("seqb")
    x_lo = a // 8
    y = lax.rem(a // 2, 4)
    core = lax.rem(a, 2)
    x_hi = b // 8
    z = lax.rem(b, 8)
    return x_hi * 2 + x_lo, y, z, core


def at(x, y, z, core):
    return (lax.rem(x, 2) * 8 + y * 2 + core, (x // 2) * 8 + z)


def along(step):
    a = lax.axis_index("seqa")
    b = lax.axis_index("seqb")
    index = lax.rem(a * 16 + b + step + 256, 256)
    return (index // 16, lax.rem(index, 16))


def meet():
    x, y, z, core = coords()
    found = [at(x, y, lax.rem(z + k, 8), core) for k in range(1, 8)]
    found += [at(lax.rem(x + k, 4), y, z, core) for k in (1, 2, 3)]
    found += [at(x, lax.rem(y + k, 4), z, core) for k in (1, 2, 3)]
    found += [at(x, y, z, 1 - core), along(1), along(-1)]
    barrier = pltpu.get_barrier_semaphore()
    for device in found:
        pl.semaphore_signal(barrier, inc=1, device_id=device, device_id_type=MESH)
    pl.semaphore_wait(barrier, len(found))


class Wire:
    def __init__(self, sems):
        self.sems, self.used, self.open = sems, 0, []

    def take(self, count):
        found = [self.sems.at[self.used + i] for i in range(count)]
        self.used += count
        return found

    def send(self, src, dst, device, leaving, landing):
        copy = pltpu.make_async_remote_copy(
            src_ref=src, dst_ref=dst, send_sem=leaving, recv_sem=landing, device_id=device, device_id_type=MESH
        )
        copy.start()
        return copy

    def alone(self, src, dst, device):
        copy = self.send(src, dst, device, *self.take(2))
        self.open.append(copy)
        return copy

    def finish(self):
        for copy in self.open:
            copy.wait_send()


def waiting(ref, sem, device):
    return pltpu.make_async_remote_copy(
        src_ref=ref, dst_ref=ref, send_sem=sem, recv_sem=sem, device_id=device, device_id_type=MESH
    )


def ends(axis):
    x, y, z, core = coords()
    p = x if axis == "x" else y
    plus, minus, opposite = lax.rem(p + 1, 4), lax.rem(p + 3, 4), lax.rem(p + 2, 4)
    if axis == "x":
        return p, plus, minus, opposite, [at(q, y, z, core) for q in (plus, minus, opposite)]
    return p, plus, minus, opposite, [at(x, q, z, core) for q in (plus, minus, opposite)]


def settle_sends(w, lanes, leaving):
    x, y, z, core = coords()
    lo, hi = lanes
    other = at(x, y, z, 1 - core)
    waiting(w.at[0, 0:3, 0, 0, :, lo:hi], leaving[0], other).wait_send()
    waiting(w.at[:, 0:3, 0, :, :, lo:hi], leaving[1], other).wait_send()


def settle_across(w, lanes, leaving):
    x, y, z, core = coords()
    waiting(w.at[:, :, core, :, :, lanes[0] : lanes[1]], leaving[2], at(x, y, z, 1 - core)).wait_send()


def gather_flow(wire, w, lanes, first, leaving, landing):
    x, y, z, core = coords()
    lo, hi = lanes
    other = at(x, y, z, 1 - core)
    near, lines, over = leaving
    from_minus, from_plus, from_far, m_own, m_minus, m_rest, p_plus, p_far, p_rest, rel_a, rel_b, home = landing
    p, plus, minus, far, (to_plus, to_minus, to_far) = ends(first)
    q, q_plus, q_minus, q_far, (up, down, _) = ends("y" if first == "x" else "x")

    def block(a, b):
        if first == "x":
            return w.at[lax.rem(a, 2), b, core, a // 2, :, lo:hi]
        return w.at[lax.rem(b, 2), a, core, b // 2, :, lo:hi]

    def line(b):
        if first == "x":
            return w.at[:, b, core, :, :, lo:hi]
        return w.at[lax.rem(b, 2), :, core, b // 2, :, lo:hi]

    def put(ref, device, leave, land):
        return wire.send(ref, ref, device, leave, land)

    two = w.at[0, 0, 0, 0:2, :, lo:hi]
    a = put(block(p, q), to_plus, near, from_minus)
    b = put(block(p, q), to_minus, near, from_plus)
    c = put(block(p, q), to_far, near, from_far)
    yield
    d = put(block(p, q), up, lines, m_own)
    put(block(p, q), down, lines, p_rest)
    put(block(p, q), other, over, home)
    yield
    a.wait_recv()
    e = put(block(minus, q), up, lines, m_minus)
    put(block(minus, q), down, lines, p_rest)
    b.wait_recv()
    f = put(block(plus, q), down, lines, p_plus)
    put(block(plus, q), up, lines, m_rest)
    c.wait_recv()
    g = put(block(far, q), down, lines, p_far)
    put(block(far, q), up, lines, m_rest)
    d.wait_recv()
    put(block(p, q_minus), up, lines, rel_a)
    for near_block in (minus, plus, far):
        put(block(near_block, q), other, over, home)
    yield
    e.wait_recv()
    put(block(minus, q_minus), up, lines, rel_a)
    f.wait_recv()
    put(block(plus, q_plus), down, lines, rel_b)
    g.wait_recv()
    put(block(far, q_plus), down, lines, rel_b)
    waiting(two, m_rest, other).wait_recv()
    put(line(q_minus), other, over, home)
    waiting(two, p_rest, other).wait_recv()
    put(line(q_plus), other, over, home)
    yield
    waiting(two, rel_a, other).wait_recv()
    waiting(two, rel_b, other).wait_recv()
    put(line(q_far), other, over, home)
    yield
    waiting(w.at[:, :, 1 - core, :, :, lo:hi], home, other).wait_recv()
    yield


def reduce_flow(wire, acc, fin, lanes, first, leaving, landing, bufs):
    s1, r1, s0, r0, s2, r2, s3, r3 = bufs
    lo, hi = lanes
    near, lines = leaving[0], leaving[1]
    p, plus, minus, far, (to_plus, to_minus, _) = ends(first)
    own, up_to, down_to, across, (up, down, over) = ends("y" if first == "x" else "x")

    def block(a, b):
        if first == "y":
            return (lax.rem(b, 2), a, b // 2, slice(None), slice(lo, hi))
        return (lax.rem(a, 2), b, a // 2, slice(None), slice(lo, hi))

    some = (down_to, own)
    rest = (across, up_to)
    for i in range(2):
        s1[0, i] = acc[block(far, some[i])].astype(BF16)
        s1[1, i] = acc[block(far, rest[i])].astype(BF16)
    a = wire.send(s1.at[0], r1.at[0], to_plus, lines, landing[0])
    b = wire.send(s1.at[1], r1.at[1], to_minus, lines, landing[1])
    yield
    for i in range(2):
        s0[0, i] = acc[block(plus, rest[i])].astype(BF16)
        s0[1, i] = acc[block(minus, some[i])].astype(BF16)
    c = wire.send(s0.at[0], r0.at[0], to_plus, lines, landing[2])
    d = wire.send(s0.at[1], r0.at[1], to_minus, lines, landing[3])
    yield
    a.wait_recv()
    for i in range(2):
        s2[0, i] = (acc[block(plus, some[i])] + r1[0, i].astype(F32)).astype(BF16)
    e = wire.send(s2.at[0], r2.at[0], to_plus, lines, landing[4])
    b.wait_recv()
    for i in range(2):
        s2[1, i] = (acc[block(minus, rest[i])] + r1[1, i].astype(F32)).astype(BF16)
    f = wire.send(s2.at[1], r2.at[1], to_minus, lines, landing[5])
    yield
    c.wait_recv()
    f.wait_recv()
    for i in range(2):
        s3[i] = (acc[block(p, rest[i])] + r0[0, i].astype(F32) + r2[1, i].astype(F32)).astype(BF16)
    a = wire.send(s3.at[0], r3.at[0], over, near, landing[6])
    b = wire.send(s3.at[1], r3.at[1], up, near, landing[7])
    d.wait_recv()
    e.wait_recv()
    s3[2] = (acc[block(p, down_to)] + r0[1, 0].astype(F32) + r2[0, 0].astype(F32)).astype(BF16)
    c = wire.send(s3.at[2], r3.at[2], down, near, landing[8])
    acc[block(p, own)] = acc[block(p, own)] + r0[1, 1].astype(F32) + r2[0, 1].astype(F32)
    yield
    a.wait_recv()
    b.wait_recv()
    c.wait_recv()
    fin[:, lo:hi] = acc[block(p, own)] + r3[0].astype(F32) + r3[1].astype(F32) + r3[2].astype(F32)
    yield


def flow_buffers(lanes):
    lo, hi = lanes
    shapes = [(2, 2, 16, hi - lo)] * 6 + [(3, 16, hi - lo)] * 2
    return [pltpu.VMEM(shape, BF16) for shape in shapes]


def step(*flows):
    for flow in flows:
        next(flow)


def kernel(ws_k, ws_v, h_in, q_in, g_in, dq, gk, gv, git, dwk, dwv, *scratch):
    (
        zgk, zgv, tk, tv, wk, wv, hto, kt, vt, qv, gvm, qa, ga, pall, ds_s, bias, dqo,
        dko, dvo, dkp, dvp, dkl, dvl, gkt, gvt, gko, gvo, acc_k, acc_v, fin_k, fin_v,
        zsk, zsv, zrk, zrv, zfk, zfv, gkr, gvr, gir, cols_v, ht, dkr, dvr,
    ) = scratch[:44]
    bufs = [scratch[44 + 8 * i : 52 + 8 * i] for i in range(8)]
    sems, local_sems = scratch[108:]
    x, y, z, core = coords()
    x_lo, x_hi = lax.rem(x, 2), x // 2
    other = at(x, y, z, 1 - core)
    before, after = along(-1), along(1)
    loads = [
        pltpu.make_async_copy(h_in, ht, local_sems.at[6]),
        pltpu.make_async_copy(q_in, qv, local_sems.at[0]),
        pltpu.make_async_copy(g_in, gvm, local_sems.at[1]),
    ]
    for copy in loads:
        copy.start()
    meet()
    wire = Wire(sems)

    k_marks = [(wire.take(3), wire.take(12)) for _ in LANES]
    v_marks = [(wire.take(3), wire.take(12)) for _ in LANES]
    z_marks = [wire.take(2) for _ in range(4)]

    def spread(src, dst, marks):
        for k in FAR:
            wire.send(src, dst.at[z], at(x, y, lax.rem(z + k, 8), core), *marks)

    spread(ws_k, zgk, z_marks[0])
    spread(ws_v, zgv, z_marks[1])
    zgk[z] = ws_k[...]
    zgv[z] = ws_v[...]

    def assemble(marks, zg, rows, w):
        waiting(zg.at[0:7], marks[1], other).wait_recv()
        for i in range(8):
            rows[2 * i : 2 * i + 2] = zg[i].astype(F32)
        w[x_lo, y, core, x_hi] = rows[...].astype(BF16)

    assemble(z_marks[0], zgk, tk, wk)
    k_in = [gather_flow(wire, wk, lanes, axis, *marks) for lanes, axis, marks in zip(LANES, FIRST, k_marks)]
    step(*k_in)
    step(*k_in)
    assemble(z_marks[1], zgv, tv, wv)
    v_in = [gather_flow(wire, wv, lanes, axis, *marks) for lanes, axis, marks in zip(LANES, FIRST, v_marks)]

    first_device = (lax.axis_index("seqa") + lax.axis_index("seqb")) == 0
    s_pos = lax.broadcasted_iota(jnp.int32, (256, 128), 0)
    t_pos = lax.broadcasted_iota(jnp.int32, (256, 128), 1)
    gap = t_pos + 128 - s_pos
    allowed = (gap >= 0) & (gap <= WIN) & (s_pos >= jnp.where(first_device, 128, 0))
    bias[...] = jnp.where(allowed, 0.0, -1e30).astype(F32)
    for copy in loads:
        copy.wait()

    def stage(j, carry):
        for src, dst in ((qv, qa), (gvm, ga)):
            rows = src[:, pl.ds(pl.multiple_of(512 * j, 512), 512)]
            for h in range(8):
                dst[j, 128 * h : 128 * h + 128] = rows[:, 64 * h : 64 * h + 64]
        return carry

    step(*k_in)
    lax.fori_loop(0, 8, stage, 0)
    step(*k_in)
    step(*v_in)
    step(*v_in)
    step(*k_in)

    def project(w, out, which):
        flat = w[:, :, which].reshape(256, D)
        rows = lax.dot_general(flat, ht[...], NN, preferred_element_type=F32)
        out[:, which, :, 128:256] = rows.astype(BF16).reshape(8, 32, 128)

    def pass_on(arr, a, b):
        return wire.alone(arr.at[a:b, :, :, 128:256], arr.at[a:b, :, :, 0:128], after)

    def pass_back(arr, dst, a, b):
        return wire.alone(arr.at[a:b], dst.at[a:b], before)

    project(wk, kt, core)
    step(*k_in)
    project(wk, kt, 1 - core)
    k_halo = [pass_on(kt, 0, 2), pass_on(kt, 2, 4)]
    step(*v_in)

    def probabilities(j):
        kj = jnp.transpose(kt[j].reshape(64, 256))
        for pair in range(4):
            both = lax.dot_general(kj, qa[j, 256 * pair : 256 * pair + 256], NT, preferred_element_type=F32)
            for h in range(2):
                s = both[:, 128 * h : 128 * h + 128] + bias[...]
                peak = jnp.max(s, axis=0, keepdims=True)
                e = jnp.exp2((s - peak) * (FACTOR * LOG2E))
                p = e * (1.0 / jnp.sum(e, axis=0, keepdims=True))
                col = 256 * pair + 128 * h
                pall[j, :, col : col + 128] = p.astype(BF16)

    def value_terms(j):
        grad = jnp.transpose(lax.dot_general(pall[j], ga[j], NN, preferred_element_type=F32))
        dvp[j] = grad[:, 0:128].astype(BF16)
        dvo[j] = grad[:, 128:256]

    def score_grads(j, ds_s):
        vj = jnp.transpose(vt[j].reshape(64, 256))
        for pair in range(4):
            both = lax.dot_general(vj, ga[j, 256 * pair : 256 * pair + 256], NT, preferred_element_type=F32)
            for h in range(2):
                col = 256 * pair + 128 * h
                gp = both[:, 128 * h : 128 * h + 128]
                p = pall[j, :, col : col + 128].astype(F32)
                delta = jnp.sum(p * gp, axis=0, keepdims=True)
                ds_s[:, col : col + 128] = (p * (gp - delta)).astype(BF16)

    def products(j, ds_s):
        k_t = kt[j].reshape(64, 256)
        turned = lax.dot_general(k_t, ds_s[...], NN, preferred_element_type=F32) * FACTOR
        for pair in range(4):
            col = 256 * pair
            two = jnp.concatenate([turned[:, col : col + 128], turned[:, col + 128 : col + 256]], axis=0)
            at_col = pl.multiple_of(512 * j + 128 * pair, 128)
            dqo[:, pl.ds(at_col, 128)] = jnp.transpose(two).astype(BF16)
        grad = jnp.transpose(lax.dot_general(ds_s[...], qa[j], NN, preferred_element_type=F32)) * FACTOR
        dkp[j] = grad[:, 0:128].astype(BF16)
        dko[j] = grad[:, 128:256]

    def forward_two(i):
        probabilities(2 * i)
        probabilities(2 * i + 1)
        value_terms(2 * i)
        value_terms(2 * i + 1)

    def backward_two(i):
        score_grads(2 * i, ds_s.at[0])
        score_grads(2 * i + 1, ds_s.at[1])
        products(2 * i, ds_s.at[0])
        products(2 * i + 1, ds_s.at[1])

    k_halo[0].wait_recv()
    k_halo.append(pass_on(kt, 4, 8))
    forward_two(0)
    k_halo[1].wait_recv()
    forward_two(1)
    step(*v_in)
    dv_halo = [pass_back(dvp, dvl, 0, 4)]
    hc = wire.alone(ht, hto, other)
    k_halo[2].wait_recv()
    forward_two(2)
    dv_halo.append(pass_back(dvp, dvl, 4, 6))
    step(*v_in)
    project(wv, vt, core)
    step(*v_in)
    project(wv, vt, 1 - core)
    v_halo = [pass_on(vt, 0, 2)]
    forward_two(3)
    dv_halo.append(pass_back(dvp, dvl, 6, 8))
    v_halo += [pass_on(vt, 2, 4), pass_on(vt, 4, 8)]

    def settle(halo, own, later, total, theirs):
        for copy in halo:
            copy.wait_recv()
        total[...] = (own[...] + later[...].astype(F32)).astype(BF16).reshape(8, 2, 32, 128)
        return wire.alone(total.at[:, 1 - core], theirs, other)

    def token_rows(total):
        return jnp.transpose(total[...].reshape(512, 128).astype(F32)).astype(BF16)

    def reduce_start(total, theirs, w, acc, fin, bufs, marks):
        left = jnp.concatenate([total[:, core].reshape(256, 128), theirs[...].reshape(256, 128)], axis=1)
        flows = []
        for i, lanes in enumerate(LANES):
            lo, hi = lanes
            right = jnp.concatenate([ht[lo:hi], hto[lo:hi]], axis=1)
            part = lax.dot_general(left, right, NT, preferred_element_type=F32)
            acc[:, :, :, :, lo:hi] = part.reshape(2, 4, 2, 16, hi - lo)
            leaving, landing = marks[i]
            settle_sends(w, lanes, leaving)
            settle_across(w, lanes, leaving)
            axis = "y" if FIRST[i] == "x" else "x"
            flows.append(reduce_flow(wire, acc, fin, lanes, axis, leaving, landing, bufs[i]))
            step(flows[-1])
        return flows

    def store(src, dst, i):
        copy = pltpu.make_async_copy(src, dst, local_sems.at[i])
        copy.start()
        stores.append(copy)

    stores = []
    v_halo[0].wait_recv()
    backward_two(0)
    v_halo[1].wait_recv()
    backward_two(1)
    dk_halo = [pass_back(dkp, dkl, 0, 4)]
    v_halo[2].wait_recv()
    backward_two(2)
    dk_halo.append(pass_back(dkp, dkl, 4, 6))
    swap_v = settle(dv_halo, dvo, dvl, gvt, gvo)
    gvr[...] = token_rows(gvt)
    store(gvr, gv, 2)
    cols_v[...] = lax.dot_general(gvr[...], wv[...].reshape(512, D), NN, preferred_element_type=F32)
    hc.wait_recv()
    swap_v.wait_recv()
    v_out = reduce_start(gvt, gvo, wk, acc_v, fin_v, bufs[0:4], k_marks)
    backward_two(3)
    dk_halo.append(pass_back(dkp, dkl, 6, 8))
    step(*v_out)
    step(*v_out)
    store(dqo, dq, 3)

    def deal(fin, zf, zs, zr, marks):
        for i in range(8):
            zf[i] = fin[2 * i : 2 * i + 2]
        zs[...] = zf[...].astype(BF16)
        for k in FAR:
            to = lax.rem(z + k, 8)
            wire.send(zs.at[to], zr.at[k - 1], at(x, y, to, core), *marks)

    def collect(marks, zf, zr, held, out, i):
        waiting(zr, marks[1], other).wait_recv()
        total = zf[z]
        for k in range(7):
            total = total + zr[k].astype(F32)
        held[...] = total * (32768.0 ** (-0.5))
        store(held, out, i)

    swap_k = settle(dk_halo, dko, dkl, gkt, gko)
    gkr[...] = token_rows(gkt)
    store(gkr, gk, 4)
    cols = cols_v[...] + lax.dot_general(gkr[...], wk[...].reshape(512, D), NN, preferred_element_type=F32)
    gir[...] = jnp.transpose(cols).astype(BF16)
    store(gir, git, 5)
    step(*v_out)
    swap_k.wait_recv()
    k_out = reduce_start(gkt, gko, wv, acc_k, fin_k, bufs[4:8], v_marks)
    step(*k_out)
    step(*v_out)
    deal(fin_v, zfv, zsv, zrv, z_marks[2])
    step(*k_out)
    step(*k_out)
    collect(z_marks[2], zfv, zrv, dvr, dwv, 7)
    step(*k_out)
    deal(fin_k, zfk, zsk, zrk, z_marks[3])
    collect(z_marks[3], zfk, zrk, dkr, dwk, 8)
    for marks, ref in zip(z_marks, (zgk, zgv, zsv, zsk)):
        waiting(ref.at[0:7], marks[0], other).wait_send()
    for lanes, marks in zip(LANES + LANES, k_marks + v_marks):
        settle_sends(wk, lanes, marks[0])
    wire.finish()
    for copy in stores:
        copy.wait()


SEMS = 8 * 15 + 8 + 2 * (3 + 3 + 3 + 4 + 2 + 1)


def fused(ws_k, ws_v, ht, queries, grad_out):
    dma = pltpu.SemaphoreType.DMA
    vm = pl.BlockSpec(memory_space=pltpu.VMEM)
    hbm = pl.BlockSpec(memory_space=pl.ANY)
    v = pltpu.VMEM
    scratch = [
        v((8, 2, D), BF16), v((8, 2, D), BF16), v((16, D), F32), v((16, D), F32),
        v((2, 4, 2, 2, 16, D), BF16), v((2, 4, 2, 2, 16, D), BF16), v((D, 128), BF16),
        v((8, 2, 32, 256), BF16), v((8, 2, 32, 256), BF16), v((128, 4096), BF16), v((128, 4096), BF16),
        v((8, 1024, 64), BF16), v((8, 1024, 64), BF16), v((8, 256, 1024), BF16), v((2, 256, 1024), BF16),
        v((256, 128), F32), v((128, 4096), BF16),
        v((8, 64, 128), F32), v((8, 64, 128), F32), v((8, 64, 128), BF16), v((8, 64, 128), BF16),
        v((8, 64, 128), BF16), v((8, 64, 128), BF16), v((8, 2, 32, 128), BF16), v((8, 2, 32, 128), BF16),
        v((8, 32, 128), BF16), v((8, 32, 128), BF16), v((2, 4, 2, 16, D), F32), v((2, 4, 2, 16, D), F32),
        v((16, D), F32), v((16, D), F32),
        v((8, 2, D), BF16), v((8, 2, D), BF16), v((7, 2, D), BF16), v((7, 2, D), BF16),
        v((8, 2, D), F32), v((8, 2, D), F32),
        v((128, 512), BF16), v((128, 512), BF16), v((D, 128), BF16), v((128, D), F32), v((D, 128), BF16), v((2, D), F32), v((2, D), F32),
        *(buf for lanes in LANES + LANES for buf in flow_buffers(lanes)),
        dma((SEMS,)), dma((9,)),
    ]
    return pl.pallas_call(
        kernel,
        out_shape=(
            jax.ShapeDtypeStruct((128, 4096), BF16),
            jax.ShapeDtypeStruct((128, 512), BF16),
            jax.ShapeDtypeStruct((128, 512), BF16),
            jax.ShapeDtypeStruct((D, 128), BF16),
            jax.ShapeDtypeStruct((2, D), F32),
            jax.ShapeDtypeStruct((2, D), F32),
        ),
        in_specs=[vm, vm, hbm, hbm, hbm],
        out_specs=(hbm,) * 6,
        scratch_shapes=scratch,
        compiler_params=pltpu.CompilerParams(collective_id=0, has_side_effects=True, vmem_limit_bytes=63 * 2**20),
        name="fused",
    )(ws_k, ws_v, ht, queries, grad_out)


PARTS = (4, 1, 1, 4, 1, 1)


def hand_over(*refs):
    ins, outs, bufs, sems = refs[:6], refs[6:12], refs[12:18], refs[18]
    fetch, put = [], []
    for i, parts in enumerate(PARTS):
        rows = ins[i].shape[0] // parts
        for part in range(parts):
            view = pl.ds(rows * part, rows)
            k = len(fetch)
            fetch.append(pltpu.make_async_copy(ins[i].at[view], bufs[i].at[view], sems.at[2 * k]))
            put.append(pltpu.make_async_copy(bufs[i].at[view], outs[i].at[view], sems.at[2 * k + 1]))
    for copy in fetch:
        copy.start()
    for k, copy in enumerate(fetch):
        copy.wait()
        put[k].start()
    for copy in put:
        copy.wait()


def published(arrays):
    hbm = pl.BlockSpec(memory_space=pl.ANY)
    return pl.pallas_call(
        hand_over,
        out_shape=tuple(jax.ShapeDtypeStruct(a.shape, a.dtype) for a in arrays),
        in_specs=[hbm] * 6,
        out_specs=(hbm,) * 6,
        scratch_shapes=[pltpu.VMEM(a.shape, a.dtype) for a in arrays] + [pltpu.SemaphoreType.DMA((2 * sum(PARTS),))],
        name="hand_over",
    )(*arrays)


def shards(hidden_in, queries, grad_out, key_weight, value_weight):
    dq, gk, gv, git, dwk, dwv = published(fused(key_weight.T, value_weight.T, hidden_in.T, queries, grad_out))
    return dq, gk, gv, git.T, dwk.T, dwv.T


def solution(mesh):
    rows = P(("seqa", "seqb"), None)
    columns = P(None, ("seqa", "seqb"))
    return jax.shard_map(
        shards,
        mesh=mesh,
        in_specs=(rows, rows, rows, columns, columns),
        out_specs=(rows, rows, rows, rows, columns, columns),
        check_vma=False,
    )
```
